256 devices in a mesh: dp: 16 (over z, core), spatial: 16 (over x, y).
Axes of the slice: x: 4, y: 4, z: 8, core: 2. Of those that a mesh axis runs over, the one named last changes fastest.
Arguments:
- fields: bfloat16 [192, 1024, 768], P('spatial', 'dp'), may hold values from -6 to 6
- filter_weight: float32 [2, 1024, 192], P(None, 'dp'), may hold values from -8 to 8
- cotangent: bfloat16 [192, 1024, 768], P('spatial', 'dp'), may hold values from -6 to 6
Outputs:
- activated: bfloat16 [192, 1024, 768], P('spatial', 'dp')
- grad_fields: bfloat16 [192, 1024, 768], P('spatial', 'dp')
- grad_weight: float32 [2, 1024, 192], P(None, 'dp')
The draws below stay inside these ranges and needn't reach their ends.
All inputs are finite; a program needn't handle non-finite values.
Results may differ from the reference program's by a relative error of at most 0.014.
Values may be sent and summed in bfloat16 or wider, within the bound.
A program may use at most 64 MiB of HBM per device.

```python
import math
import jax
import jax.numpy as jnp
from jax import lax

C = 1024
NLON = 768
NLAT = 192
MODES = 192


def level_of(key, extent, cuts, low, high):
    factor_of, own = 1.0, jax.random.fold_in(key, 6)
    for axis_at, blocks in cuts:
        steps = jnp.exp(jax.random.uniform(jax.random.fold_in(own, axis_at), (blocks,), jnp.float32, low / len(cuts), high / len(cuts)))
        factor_of = factor_of * jnp.repeat(steps, extent[axis_at] // blocks).reshape([-1 if axis == axis_at else 1 for axis in range(len(extent))])
    return factor_of


def bell_draw(rng, shape, scale, bound, pieces=(), kind=jnp.bfloat16):
    loudness = level_of(rng, shape, pieces, -0.22, 0.18) if pieces else 1.0
    drawn = jax.random.normal(rng, shape, jnp.float32) * scale * loudness
    return jnp.minimum(jnp.maximum(drawn, -bound), bound).astype(kind)


def setup_inputs(seed: int = 0) -> dict:
    streams_of = jax.random.split(jax.random.key(seed), 4)
    return {
        "fields": bell_draw(streams_of[0], (NLAT, C, NLON), 1.0, 6.0, ((0, 16), (1, 16))),
        "filter_weight": bell_draw(streams_of[1], (2, C, MODES), 2.0, 8.0, ((1, 16),), jnp.float32),
        "cotangent": bell_draw(streams_of[2], (NLAT, C, NLON), 1.0, 6.0, ((0, 16), (1, 16))),
    }


def legendre_rows(first_mode, count, degrees, nlat, modes):
    rows = jnp.arange(nlat).astype(jnp.float32)
    theta = math.pi * (rows + 0.5) / nlat
    cosine = jnp.cos(theta)
    sine = jnp.sin(theta)

    def diag_step(carry, order):
        order_f = order.astype(jnp.float32)
        factor = jnp.sqrt((2.0 * order_f + 1.0) / jnp.maximum(2.0 * order_f, 1.0))
        value = jnp.where(order > 0, -factor * sine * carry, carry)
        return (value, value)
    start = jnp.full((nlat,), 1.0 / math.sqrt(4.0 * math.pi), jnp.float32)
    _, diagonal = lax.scan(diag_step, start, jnp.arange(modes, dtype=jnp.int32))
    chosen = lax.dynamic_slice_in_dim(diagonal, first_mode, count, 0)
    orders = (first_mode + jnp.arange(count, dtype=jnp.int32))[:, None]
    order_f = orders.astype(jnp.float32)

    def degree_step(carry, degree):
        previous, before = carry
        deg_f = degree.astype(jnp.float32)
        scale_now = jnp.sqrt(jnp.maximum(4.0 * deg_f * deg_f - 1.0, 1.0) / jnp.maximum(deg_f * deg_f - order_f * order_f, 1.0))
        last_f = deg_f - 1.0
        scale_last = jnp.sqrt(jnp.maximum(4.0 * last_f * last_f - 1.0, 1.0) / jnp.maximum(last_f * last_f - order_f * order_f, 1.0))
        general = scale_now * (cosine * previous - before / scale_last)
        first_up = jnp.sqrt(2.0 * order_f + 3.0) * cosine * chosen
        value = jnp.where(degree < orders, jnp.zeros_like(general), jnp.where(degree == orders, chosen, jnp.where(degree == orders + 1, first_up, general)))
        return ((value, previous), value)
    zeros = jnp.zeros((count, nlat), jnp.float32)
    _, table = lax.scan(degree_step, (zeros, zeros), jnp.arange(degrees, dtype=jnp.int32))
    return jnp.transpose(table, (1, 0, 2))

def fourier_tables(nlon, modes):
    points = jnp.arange(nlon, dtype=jnp.int32)[:, None]
    orders = jnp.arange(modes, dtype=jnp.int32)[None, :]
    angle = 2.0 * math.pi / nlon * (points * orders % nlon).astype(jnp.float32)
    cosine = jnp.cos(angle)
    sine = jnp.sin(angle)
    step_size = 2.0 * math.pi / nlon
    forward = jnp.stack([step_size * cosine, -step_size * sine], axis=2).reshape(nlon, 2 * modes)
    factor = jnp.where(orders == 0, 1.0, 2.0).astype(jnp.float32)
    inverse = jnp.stack([factor * cosine, -factor * sine], axis=2).reshape(nlon, 2 * modes)
    return (forward.astype(jnp.bfloat16), inverse.astype(jnp.bfloat16))

def reference(fields, filter_weight, cotangent):
    nlat, width, nlon = fields.shape
    modes = nlat
    highest = lax.Precision.HIGHEST
    forward, inverse = fourier_tables(nlon, modes)
    forward_f = forward.astype(jnp.float32)
    inverse_f = inverse.astype(jnp.float32)
    table = legendre_rows(0, modes, modes, nlat, modes)
    rows = jnp.arange(nlat).astype(jnp.float32)
    quad_w = math.pi / nlat * jnp.sin(math.pi * (rows + 0.5) / nlat)
    quad = table * quad_w
    group = math.gcd(width, 128)
    blocks = width // group

    def one_block(inputs):
        sample, slope_in, weight = inputs
        wr = weight[0][None, :, :]
        wi = weight[1][None, :, :]
        spectra = jnp.einsum('jcn,nk->kcj', sample.astype(jnp.float32), forward_f, precision=highest).astype(jnp.bfloat16)
        split = spectra.astype(jnp.float32).reshape(modes, 2, group, nlat)
        coeffs = jnp.einsum('mlj,mpcj->mpcl', quad, split, precision=highest)
        real_c, imag_c = (coeffs[:, 0], coeffs[:, 1])
        filtered = jnp.stack([wr * real_c - wi * imag_c, wr * imag_c + wi * real_c], axis=1)
        synth = jnp.einsum('mlj,mpcl->mpcj', table, filtered, precision=highest).reshape(2 * modes, group, nlat).astype(jnp.bfloat16)
        pre = jnp.einsum('kcj,nk->jcn', synth.astype(jnp.float32), inverse_f, precision=highest)
        cdf = 0.5 * (1.0 + lax.erf(pre / math.sqrt(2.0)))
        density = jnp.exp(-0.5 * pre * pre) / math.sqrt(2.0 * math.pi)
        activated = (pre * cdf).astype(jnp.bfloat16)
        dpre = (slope_in.astype(jnp.float32) * (cdf + pre * density)).astype(jnp.bfloat16)
        dsynth = jnp.einsum('jcn,nk->kcj', dpre.astype(jnp.float32), inverse_f, precision=highest).astype(jnp.bfloat16)
        dsplit = dsynth.astype(jnp.float32).reshape(modes, 2, group, nlat)
        dfiltered = jnp.einsum('mlj,mpcj->mpcl', table, dsplit, precision=highest)
        real_d, imag_d = (dfiltered[:, 0], dfiltered[:, 1])
        grad_real = lax.optimization_barrier(jnp.sum(real_d * real_c + imag_d * imag_c, axis=0))
        grad_imag = lax.optimization_barrier(jnp.sum(imag_d * real_c - real_d * imag_c, axis=0))
        grad_block = jnp.stack([grad_real, grad_imag], axis=0) / modes
        dcoeffs = jnp.stack([wr * real_d + wi * imag_d, wr * imag_d - wi * real_d], axis=1)
        dspectra = jnp.einsum('mlj,mpcl->mpcj', quad, dcoeffs, precision=highest).reshape(2 * modes, group, nlat).astype(jnp.bfloat16)
        grad_fields = jnp.einsum('kcj,nk->jcn', dspectra.astype(jnp.float32), forward_f, precision=highest).astype(jnp.bfloat16)
        return (activated, grad_fields, grad_block)
    field_blocks = jnp.transpose(fields.reshape(nlat, blocks, group, nlon), (1, 0, 2, 3))
    slope_blocks = jnp.transpose(cotangent.reshape(nlat, blocks, group, nlon), (1, 0, 2, 3))
    weight_blocks = jnp.transpose(filter_weight.reshape(2, blocks, group, modes), (1, 0, 2, 3))
    activated, grad_fields, grad_weight = lax.map(one_block, (field_blocks, slope_blocks, weight_blocks))
    activated = jnp.transpose(activated, (1, 0, 2, 3)).reshape(nlat, width, nlon)
    grad_fields = jnp.transpose(grad_fields, (1, 0, 2, 3)).reshape(nlat, width, nlon)
    grad_weight = jnp.transpose(grad_weight, (1, 0, 2, 3)).reshape(2, width, modes)
    return (activated, grad_fields, grad_weight)
```

```python
import functools
import math

import jax
import jax.numpy as jnp
import ml_dtypes
import numpy as np
from jax import lax
from jax.sharding import PartitionSpec as P


@functools.lru_cache(None)
def legendre_table(nlat):
    theta = np.pi * (np.arange(nlat) + 0.5) / nlat
    cosine, sine = np.cos(theta), np.sin(theta)
    table = np.zeros((nlat, nlat, nlat))
    diagonal = np.full((nlat,), 1.0 / math.sqrt(4.0 * math.pi))
    for m in range(nlat):
        if m:
            diagonal = -math.sqrt((2.0 * m + 1.0) / (2.0 * m)) * sine * diagonal
        table[m, m] = diagonal
        if m + 1 < nlat:
            table[m, m + 1] = math.sqrt(2.0 * m + 3.0) * cosine * diagonal
    orders = np.arange(nlat)
    for l in range(2, nlat):
        m = orders[: l - 1, None].astype(np.float64)
        scale = np.sqrt((4.0 * l * l - 1.0) / (l * l - m * m))
        last = np.sqrt((4.0 * (l - 1) ** 2 - 1.0) / ((l - 1) ** 2 - m * m))
        table[: l - 1, l] = scale * (cosine * table[: l - 1, l - 1] - table[: l - 1, l - 2] / last)
    return table


@functools.lru_cache(None)
def fourier_tables(nlon, modes):
    points, orders = np.arange(nlon)[:, None], np.arange(modes)[None, :]
    angle = 2.0 * np.pi / nlon * (points * orders % nlon)
    parts = np.stack([np.cos(angle), -np.sin(angle)], axis=1)
    factor = np.where(orders == 0, 1.0, 2.0)[:, None]
    forward = (2.0 * np.pi / nlon * parts).astype(ml_dtypes.bfloat16)
    inverse = (factor * parts).astype(ml_dtypes.bfloat16)
    return forward, inverse


def shards(fields, filter_weight, cotangent):
    lat_rows, width, nlon = fields.shape
    spatial = lax.axis_size("spatial")
    nlat = lat_rows * spatial
    me = lax.axis_index("spatial")
    f32, bf16 = jnp.float32, jnp.bfloat16
    forward, inverse = (
        jnp.asarray(t.transpose(0, 2, 1).reshape(nlon, 2 * nlat)) for t in fourier_tables(nlon, nlat)
    )
    tables = legendre_table(nlat).reshape(spatial, lat_rows, nlat, nlat).astype(ml_dtypes.bfloat16)
    table = lax.dynamic_index_in_dim(jnp.asarray(tables), me, 0, keepdims=False)
    quad_w = (np.pi / nlat * np.sin(np.pi * (np.arange(nlat) + 0.5) / nlat)).astype(np.float32)
    own_w = lax.dynamic_slice_in_dim(jnp.asarray(quad_w), me * lat_rows, lat_rows, 0)
    wr, wi = filter_weight[0][None], filter_weight[1][None]
    dot = functools.partial(jnp.einsum, preferred_element_type=f32)

    spectra = (dot("jcn,nk->kcj", fields, forward) * own_w).astype(bf16)
    split = lax.all_to_all(spectra, "spatial", split_axis=0, concat_axis=2, tiled=True)
    split = split.reshape(lat_rows, 2, width, nlat)
    coeffs = dot("mlj,mpcj->mpcl", table, split)
    real_c, imag_c = coeffs[:, 0], coeffs[:, 1]
    filtered = jnp.stack([wr * real_c - wi * imag_c, wr * imag_c + wi * real_c], axis=1)
    synth = dot("mlj,mpcl->mpcj", table, filtered.astype(bf16)).reshape(2 * lat_rows, width, nlat)
    rows = lax.all_to_all(synth.astype(bf16), "spatial", split_axis=2, concat_axis=0, tiled=True)
    pre = dot("kcj,nk->jcn", rows, inverse)
    cdf = 0.5 * (1.0 + lax.erf(pre / math.sqrt(2.0)))
    density = jnp.exp(-0.5 * pre * pre) / math.sqrt(2.0 * math.pi)
    activated = (pre * cdf).astype(bf16)
    dpre = (cotangent.astype(f32) * (cdf + pre * density)).astype(bf16)
    dsynth = dot("jcn,nk->kcj", dpre, inverse).astype(bf16)
    dsplit = lax.all_to_all(dsynth, "spatial", split_axis=0, concat_axis=2, tiled=True)
    dsplit = dsplit.reshape(lat_rows, 2, width, nlat)
    dfiltered = dot("mlj,mpcj->mpcl", table, dsplit)
    real_d, imag_d = dfiltered[:, 0], dfiltered[:, 1]
    grad_real = jnp.sum(real_d * real_c + imag_d * imag_c, axis=0)
    grad_imag = jnp.sum(imag_d * real_c - real_d * imag_c, axis=0)
    partial_grad = jnp.stack([grad_real, grad_imag], axis=0).astype(bf16)
    dcoeffs = jnp.stack([wr * real_d + wi * imag_d, wr * imag_d - wi * real_d], axis=1)
    dspectra = dot("mlj,mpcl->mpcj", table, dcoeffs.astype(bf16)) * quad_w
    dspectra = dspectra.reshape(2 * lat_rows, width, nlat).astype(bf16)
    drows = lax.all_to_all(dspectra, "spatial", split_axis=2, concat_axis=0, tiled=True)
    grad_fields = dot("kcj,nk->jcn", drows, forward).astype(bf16)

    pieces = partial_grad.reshape(2, spatial, width // spatial, nlat).transpose(1, 0, 2, 3)
    pieces = lax.all_to_all(pieces, "spatial", split_axis=0, concat_axis=0, tiled=True)
    owned = (jnp.sum(pieces.astype(f32), axis=0) / nlat).astype(bf16)
    owned = jnp.broadcast_to(owned[None], (spatial,) + owned.shape)
    whole = lax.all_to_all(owned, "spatial", split_axis=0, concat_axis=0, tiled=True)
    grad_weight = whole.transpose(1, 0, 2, 3).reshape(2, width, nlat).astype(f32)
    return activated, grad_fields, grad_weight


def solution(mesh):
    in_specs = (P("spatial", "dp", None), P(None, "dp", None), P("spatial", "dp", None))
    out_specs = (P("spatial", "dp", None), P("spatial", "dp", None), P(None, "dp", None))
    return jax.shard_map(shards, mesh=mesh, in_specs=in_specs, out_specs=out_specs, check_vma=False)
```

```python
import functools
import math

import jax
import jax.numpy as jnp
import ml_dtypes
import numpy as np
from jax import lax
from jax.experimental import pallas as pl
from jax.experimental.pallas import tpu as pltpu
from jax.sharding import PartitionSpec as P

MESH = pl.DeviceIdType.MESH
F32, BF16 = jnp.float32, jnp.bfloat16

N = 16
ROWS = 12
WIDTH = 64
NLAT = N * ROWS
NLON = 768
GROUPS, TILES = 3, 3
FULL = N * GROUPS * TILES
REST = N * GROUPS
BLOCK = GROUPS * TILES * 16


@functools.lru_cache(None)
def constants():
    f32, bf16 = np.float32, ml_dtypes.bfloat16
    full = [ROWS * d + 4 * g + t for d in range(N) for g in range(GROUPS) for t in range(TILES)]
    rest = [ROWS * d + 4 * g + 3 for d in range(N) for g in range(GROUPS)]
    orders = np.array(full + rest)
    angle = 2.0 * np.pi / NLON * (orders[:, None] * np.arange(NLON)[None, :] % NLON)
    parts = np.concatenate([np.cos(angle), -np.sin(angle)], axis=0)
    factor = np.where(orders == 0, 1.0, 2.0)[:, None]
    forward = (2.0 * np.pi / NLON * parts).astype(bf16)
    inverse = (np.concatenate([factor, factor], axis=0) * parts).astype(bf16)

    theta = np.pi * (np.arange(NLAT) + 0.5) / NLAT
    cosine, sine = np.cos(theta), np.sin(theta)
    weights = np.pi / NLAT * sine
    row_weights = np.zeros((N, 16, 128), f32)
    row_weights[:, :ROWS] = weights.reshape(N, ROWS, 1)

    lane = np.arange(256)
    s, r = lane // 16, lane % 16
    own = r < ROWS
    rows_of = [np.where(own, ROWS * s + r, ROWS * s + 4 * t + r - ROWS) for t in range(TILES)]
    col_weights = np.stack([np.repeat(weights[j][:, None], 128, 1) for j in rows_of]).astype(f32)

    diagonal = np.zeros((NLAT, NLAT))
    diagonal[0] = 1.0 / math.sqrt(4.0 * math.pi)
    for m in range(1, NLAT):
        diagonal[m] = -math.sqrt((2.0 * m + 1.0) / (2.0 * m)) * sine * diagonal[m - 1]
    m, l = np.arange(NLAT)[:, None].astype(float), np.arange(NLAT)[None, :].astype(float)
    above = l > m
    scale = np.where(above, np.sqrt(np.where(above, 4 * l * l - 1, 1.0) / np.where(above, l * l - m * m, 1.0)), 0.0)
    last = l - 1
    two = last > m
    scale_last = np.sqrt(np.where(two, 4 * last * last - 1, 1.0) / np.where(two, last * last - m * m, 1.0))
    back = np.where(two, scale / scale_last, 0.0)

    cos_map = np.zeros((16, 256), f32)
    order_map = np.full((16, 256), -1.0, f32)
    diag_map = np.zeros((N, 16, 256), f32)
    coef = np.zeros((N, 64, 256), f32)
    for g in range(GROUPS):
        for t in range(TILES):
            v = TILES * g + t
            cos_map[v] = cosine[rows_of[t]]
            order_map[v] = np.where(own, 4 * g + t, 4 * g + 3)
            for d in range(N):
                ma, mb = ROWS * d + 4 * g + t, ROWS * d + 4 * g + 3
                diag_map[d, v] = np.where(own, diagonal[ma][rows_of[t]], diagonal[mb][rows_of[t]])
                for kind, values in enumerate((scale[ma], scale[mb], back[ma], back[mb])):
                    coef[d, 16 * kind + v, :NLAT] = values
    maps = np.concatenate([cos_map, order_map], axis=0)
    return dict(
        forward=forward, inverse=inverse, row_weights=row_weights, col_weights=col_weights,
        maps=maps, diag=diag_map, coef=coef,
    )


def kernel(
    x_hbm, cot_hbm, weight_hbm, ft_hbm, gt_hbm, roww_hbm, colw_hbm, maps_hbm, diag_hbm, coef_hbm,
    act_hbm, gf_hbm, gw_hbm,
    xv, cotv, weightv, ftv, gtv, rowwv, colwv, mapsv, diagv, coefv,
    stage, send, recv, legendre0, legendre1, table, table_t, coeffs, rotated, prev, tt, actv, dprev,
    gsend, grecv, gout, gall, sums, gwv,
    load_sem, store_sem, send_a, recv_a, send_g, recv_g, send_r, recv_r,
):
    dp, me = lax.axis_index("dp"), lax.axis_index("spatial")
    peer_of = lambda s: lax.rem(me + s, N)

    loads = [
        pltpu.make_async_copy(src, dst, load_sem.at[i])
        for i, (src, dst) in enumerate((
            (x_hbm, xv), (ft_hbm, ftv), (roww_hbm.at[me], rowwv), (coef_hbm.at[me], coefv),
            (diag_hbm.at[me], diagv), (maps_hbm, mapsv), (weight_hbm, weightv), (gt_hbm, gtv),
            (cot_hbm, cotv), (colw_hbm, colwv),
        ))
    ]
    for load in loads:
        load.start()

    barrier = pltpu.get_barrier_semaphore()

    def greet(s, _):
        pl.semaphore_signal(barrier, inc=1, device_id=(dp, peer_of(s)), device_id_type=MESH)
        return 0

    lax.fori_loop(1, N, greet, 0)

    low = lax.broadcasted_iota(jnp.int32, (1, 128), 1) < WIDTH
    half = lambda value: pltpu.roll(value, WIDTH, 1)

    def whole_copy(phase, peer):
        return pltpu.make_async_remote_copy(
            src_ref=send.at[phase, peer], dst_ref=recv.at[phase, me],
            send_sem=send_a.at[phase, peer], recv_sem=recv_a.at[phase, me],
            device_id=(dp, peer), device_id_type=MESH,
        )

    def whole_arrival(phase, src):
        return pltpu.make_async_remote_copy(
            src_ref=recv.at[phase, src], dst_ref=recv.at[phase, src],
            send_sem=send_a.at[phase, src], recv_sem=recv_a.at[phase, src],
            device_id=(dp, src), device_id_type=MESH,
        )

    def group_rows(g):
        return pl.ds(pl.multiple_of(g * 48, 48), 48)

    def group_copy(phase, g, peer):
        return pltpu.make_async_remote_copy(
            src_ref=send.at[phase, peer, group_rows(g)], dst_ref=recv.at[phase, me, group_rows(g)],
            send_sem=send_g.at[phase // 2, g, peer], recv_sem=recv_g.at[phase // 2, g, me],
            device_id=(dp, peer), device_id_type=MESH,
        )

    def group_arrival(phase, g, src):
        ref = recv.at[phase, src, group_rows(g)]
        return pltpu.make_async_remote_copy(
            src_ref=ref, dst_ref=ref,
            send_sem=send_g.at[phase // 2, g, src], recv_sem=recv_g.at[phase // 2, g, src],
            device_id=(dp, src), device_id_type=MESH,
        )

    def fourier(q, rows_ref, factors, scaled):
        block = rows_ref[pl.ds(pl.multiple_of(q * 256, 256), 256), :]
        out = lax.dot_general(factors[...], block, (((1,), (1,)), ((), ())), preferred_element_type=F32)
        for u in range(2):
            real, imag = out[:NLAT, 128 * u : 128 * u + 128], out[NLAT:, 128 * u : 128 * u + 128]
            pair = (jnp.where(low, real, half(imag)), jnp.where(low, half(real), imag))
            for i, value in enumerate(pair):
                j = 4 * q + 2 * u + i
                if scaled:
                    value = value * rowwv[pl.ds(j, 1), :]
                stage[pl.ds(j, FULL, stride=16), :] = value[:FULL]
                stage[pl.ds(q * 16 + ROWS + 2 * u + i, REST, stride=48), :] = value[FULL:]
        return 0

    def ship(phase):
        recv[phase, me] = stage[pl.ds(pl.multiple_of(me * BLOCK, BLOCK), BLOCK), :].astype(BF16)

        def one(s, _):
            peer = peer_of(s)
            send[phase, peer] = stage[pl.ds(pl.multiple_of(peer * BLOCK, BLOCK), BLOCK), :].astype(BF16)
            whole_copy(phase, peer).start()
            return 0

        lax.fori_loop(1, N, one, 0)

    def each_peer(action):
        def one(s, _):
            action(peer_of(s))
            return 0

        lax.fori_loop(1, N, one, 0)

    for load in loads[:3]:
        load.wait()
    lax.fori_loop(0, 3, lambda q, _: fourier(q, xv, ftv, True), 0)
    pl.semaphore_wait(barrier, N - 1)
    ship(0)

    for load in loads[3:]:
        load.wait()
    own_lane = lax.broadcasted_iota(jnp.int32, (1, 128), 1) % 16 < ROWS
    first = (ROWS * me).astype(F32)

    for h in range(2):
        def degrees(g, carry, h=h):
            shift = lax.rem(128 - 8 * g, 128)
            turned = pltpu.roll(coefv[:, 128 * h : 128 * h + 128], shift, 1)
            for i in range(8):
                l = 128 * h + 8 * g + i
                pick = lambda kind: jnp.broadcast_to(turned[16 * kind : 16 * kind + 16, i : i + 1], (16, 128))
                scale = jnp.where(own_lane, pick(0), pick(1))
                back = jnp.where(own_lane, pick(2), pick(3))
                new = []
                for u, store in ((0, legendre0), (1, legendre1)):
                    cols = slice(128 * u, 128 * u + 128)
                    last, before = carry[2 * u], carry[2 * u + 1]
                    start = jnp.where(mapsv[16:, cols] + first == l.astype(F32), diagv[:, cols], 0.0)
                    value = (scale * mapsv[:16, cols]) * last + (start - back * before)
                    store[pl.ds(l, 16, stride=NLAT), :] = value
                    new += [value, last]
                carry = tuple(new)
            return carry

        if h == 0:
            carry = (jnp.zeros((16, 128), F32),) * 4
        carry = lax.fori_loop(0, 16 if h == 0 else 8, degrees, carry)

    def finish(v, _):
        rows = pl.ds(pl.multiple_of(v * NLAT, NLAT), NLAT)
        for u, store in ((0, legendre0), (1, legendre1)):
            part = store[rows, :].astype(BF16)
            table[v, :, 128 * u : 128 * u + 128] = part
            table_t[v, 128 * u : 128 * u + 128, :] = part.T
        return 0

    lax.fori_loop(0, GROUPS * TILES, finish, 0)

    weights = weightv[...].T
    filt = jnp.where(low, weights, half(weights))
    rotated[0] = filt
    filt = jnp.where(low, -half(weights), weights)
    rotated[1] = filt

    own_row = lax.broadcasted_iota(jnp.int32, (256, 128), 0) % 16 < ROWS

    def analyse(phase, g):
        found, fourth = [], None
        for t in range(TILES):
            rows = pl.ds(pl.multiple_of((TILES * g + t) * 16, 16), 16)
            block = recv[phase, :, rows, :].reshape(256, 128)
            zero = jnp.zeros_like(block)
            both = jnp.concatenate([jnp.where(own_row, block, zero), jnp.where(own_row, zero, block)], axis=1)
            out = jnp.dot(table[TILES * g + t], both, preferred_element_type=F32)
            found.append(out[:, :128])
            fourth = out[:, 128:] if fourth is None else fourth + out[:, 128:]
        return found + [fourth]

    def synthesize(phase, g, values, scaled):
        for t in range(TILES):
            both = jnp.concatenate([values[t], values[3]], axis=1)
            out = jnp.dot(table_t[TILES * g + t], both, preferred_element_type=F32)
            out = jnp.where(own_row, out[:, :128], out[:, 128:])
            if scaled:
                out = out * colwv[t]
            rows = pl.ds(pl.multiple_of((TILES * g + t) * 16, 16), 16)
            send[phase, :, rows, :] = out.astype(BF16).reshape(N, 16, 128)
        each_peer(lambda peer: group_copy(phase, g, peer).start())
        recv[phase, me, group_rows(g), :] = send[phase, me, group_rows(g), :]

    each_peer(lambda src: whole_arrival(0, src).wait_recv())

    def forward_group(g, _):
        values = []
        for i, value in enumerate(analyse(0, g)):
            coeffs[4 * g + i] = value
            values.append((rotated[0] * value + rotated[1] * half(value)).astype(BF16))
        synthesize(1, g, values, False)
        return 0

    lax.fori_loop(0, GROUPS, forward_group, 0)

    def gather(phase):
        def one(s, _):
            src = peer_of(s)

            @pl.when(s > 0)
            def _():
                for g in range(GROUPS):
                    group_arrival(phase, g, src).wait_recv()

            stage[pl.ds(pl.multiple_of(src * BLOCK, BLOCK), BLOCK), :] = recv[phase, src].astype(F32)
            return 0

        lax.fori_loop(0, N, one, 0)

        def spread(j, _):
            full = stage[pl.ds(j, FULL, stride=16), :]
            rest = stage[pl.ds((j // 4) * 16 + ROWS + lax.rem(j, 4), REST, stride=48), :]
            turned = jnp.concatenate([full, rest], axis=0).astype(BF16).T
            rows = pl.ds(pl.multiple_of(j * WIDTH, WIDTH), WIDTH)
            tt[0, rows, :] = turned[:WIDTH]
            tt[1, rows, :] = turned[WIDTH:]
            return 0

        lax.fori_loop(0, ROWS, spread, 0)

    def grid_rows(q, factors):
        rows = pl.ds(pl.multiple_of(q * 256, 256), 256)
        return jnp.dot(tt[0, rows, :], factors[:NLAT, :], preferred_element_type=F32) + jnp.dot(
            tt[1, rows, :], factors[NLAT:, :], preferred_element_type=F32
        )

    gather(1)

    def activation(q, _):
        prev[...] = grid_rows(q, gtv)

        def strip(i, _):
            here = pl.ds(pl.multiple_of(i * 16, 16), 16)
            there = pl.ds(pl.multiple_of(q * 256 + i * 16, 16), 16)
            pre = prev[here, :]
            cdf = 0.5 + 0.5 * lax.erf(pre * (1.0 / math.sqrt(2.0)))
            density = jnp.exp(-0.5 * pre * pre) * (1.0 / math.sqrt(2.0 * math.pi))
            actv[there, :] = (pre * cdf).astype(BF16)
            dprev[there, :] = (cotv[there, :].astype(F32) * (cdf + pre * density)).astype(BF16)
            return 0

        lax.fori_loop(0, 16, strip, 0)
        return fourier(q, dprev, gtv, False)

    lax.fori_loop(0, 3, activation, 0)
    ship(2)
    act_store = pltpu.make_async_copy(actv, act_hbm, store_sem.at[0])
    act_store.start()

    sums[...] = jnp.zeros_like(sums)
    each_peer(lambda src: whole_arrival(2, src).wait_recv())

    def backward_group(g, _):
        values = []
        for i, value in enumerate(analyse(2, g)):
            coeff, turned = coeffs[4 * g + i], half(value)
            sums[0] = sums[0] + value * coeff
            sums[1] = sums[1] + value * half(coeff)
            values.append((rotated[0] * value - rotated[1] * turned).astype(BF16))
        synthesize(3, g, values, True)
        return 0

    lax.fori_loop(0, GROUPS, backward_group, 0)

    same, cross = sums[0], sums[1]
    partial = jnp.where(low, same + half(same), cross - half(cross)).astype(BF16)
    gsend[:ROWS] = partial.reshape(ROWS, 16, 128)
    gsend[ROWS:] = jnp.zeros((N - ROWS, 16, 128), BF16)

    def sum_copy(peer):
        return pltpu.make_async_remote_copy(
            src_ref=gsend.at[peer], dst_ref=grecv.at[me], send_sem=send_r.at[0, peer], recv_sem=recv_r.at[0, me],
            device_id=(dp, peer), device_id_type=MESH,
        )

    def sum_arrival(src):
        return pltpu.make_async_remote_copy(
            src_ref=grecv.at[src], dst_ref=grecv.at[src], send_sem=send_r.at[0, src], recv_sem=recv_r.at[0, src],
            device_id=(dp, src), device_id_type=MESH,
        )

    def all_copy(peer):
        return pltpu.make_async_remote_copy(
            src_ref=gout, dst_ref=gall.at[me], send_sem=send_r.at[1, peer], recv_sem=recv_r.at[1, me],
            device_id=(dp, peer), device_id_type=MESH,
        )

    def all_arrival(src):
        return pltpu.make_async_remote_copy(
            src_ref=gall.at[src], dst_ref=gall.at[src], send_sem=send_r.at[1, src], recv_sem=recv_r.at[1, src],
            device_id=(dp, src), device_id_type=MESH,
        )

    each_peer(lambda peer: sum_copy(peer).start())
    grecv[me] = gsend[me]
    each_peer(lambda src: sum_arrival(src).wait_recv())
    total = jnp.sum(grecv[...].astype(F32), axis=0) * (1.0 / NLAT)
    gout[...] = total.astype(BF16)
    gall[me] = total.astype(BF16)
    each_peer(lambda peer: all_copy(peer).start())

    gather(3)

    def gradient(q, _):
        rows = pl.ds(pl.multiple_of(q * 256, 256), 256)
        xv[rows, :] = grid_rows(q, ftv).astype(BF16)
        pltpu.make_async_copy(xv.at[rows], gf_hbm.at[rows], store_sem.at[2 + q]).start()
        return 0

    lax.fori_loop(0, 3, gradient, 0)

    each_peer(lambda src: all_arrival(src).wait_recv())
    gwv[...] = gall[:ROWS].reshape(NLAT, 128).astype(F32).T
    gw_store = pltpu.make_async_copy(gwv, gw_hbm, store_sem.at[1])
    gw_store.start()

    def drain(s, _):
        peer = peer_of(s)
        for phase in (0, 2):
            whole_copy(phase, peer).wait_send()
        for phase in (1, 3):
            for g in range(GROUPS):
                group_copy(phase, g, peer).wait_send()
        sum_copy(peer).wait_send()
        all_copy(peer).wait_send()
        return 0

    lax.fori_loop(1, N, drain, 0)
    act_store.wait()
    gw_store.wait()
    for q in range(3):
        rows = pl.ds(q * 256, 256)
        pltpu.make_async_copy(xv.at[rows], gf_hbm.at[rows], store_sem.at[2 + q]).wait()


def shards(fields, filter_weight, cotangent):
    rows, width, nlon = fields.shape
    if (rows, width, nlon) != (ROWS, WIDTH, NLON) or lax.axis_size("spatial") != N:
        raise ValueError("unexpected sizes")
    held = constants()
    names = ("forward", "inverse", "row_weights", "col_weights", "maps", "diag", "coef")
    flat = rows * width
    dma, vmem = pltpu.SemaphoreType.DMA, pltpu.VMEM
    activated, grad_fields, grad_weight = pl.pallas_call(
        kernel,
        out_shape=(
            jax.ShapeDtypeStruct((flat, nlon), BF16),
            jax.ShapeDtypeStruct((flat, nlon), BF16),
            jax.ShapeDtypeStruct((2 * width, NLAT), F32),
        ),
        in_specs=[pl.BlockSpec(memory_space=pl.ANY)] * 10,
        out_specs=(pl.BlockSpec(memory_space=pl.ANY),) * 3,
        scratch_shapes=[
            vmem((flat, nlon), BF16), vmem((flat, nlon), BF16), vmem((2 * width, NLAT), F32),
            vmem((2 * NLAT, nlon), BF16), vmem((2 * NLAT, nlon), BF16), vmem((16, 128), F32),
            vmem((TILES, 256, 128), F32), vmem((32, 256), F32), vmem((16, 256), F32), vmem((64, 256), F32),
            vmem((N * BLOCK, 128), F32), vmem((4, N, BLOCK, 128), BF16), vmem((4, N, BLOCK, 128), BF16),
            vmem((16 * NLAT, 128), F32), vmem((16 * NLAT, 128), F32),
            vmem((GROUPS * TILES, NLAT, 256), BF16), vmem((GROUPS * TILES, 256, NLAT), BF16),
            vmem((ROWS, NLAT, 128), F32), vmem((2, NLAT, 128), F32), vmem((256, nlon), F32),
            vmem((2, flat, NLAT), BF16), vmem((flat, nlon), BF16), vmem((flat, nlon), BF16),
            vmem((N, 16, 128), BF16), vmem((N, 16, 128), BF16), vmem((16, 128), BF16), vmem((N, 16, 128), BF16),
            vmem((2, NLAT, 128), F32), vmem((2 * width, NLAT), F32),
            dma((10,)), dma((5,)), dma((4, N)), dma((4, N)), dma((2, GROUPS, N)), dma((2, GROUPS, N)),
            dma((2, N)), dma((2, N)),
        ],
        compiler_params=pltpu.CompilerParams(
            collective_id=0, has_side_effects=True, vmem_limit_bytes=56 << 20
        ),
    )(
        fields.reshape(flat, nlon), cotangent.reshape(flat, nlon), filter_weight.reshape(2 * width, NLAT),
        *(jnp.asarray(held[name]) for name in names),
    )
    return (
        activated.reshape(rows, width, nlon), grad_fields.reshape(rows, width, nlon),
        grad_weight.reshape(2, width, NLAT),
    )


def solution(mesh):
    in_specs = (P("spatial", "dp", None), P(None, "dp", None), P("spatial", "dp", None))
    out_specs = (P("spatial", "dp", None), P("spatial", "dp", None), P(None, "dp", None))
    return jax.shard_map(shards, mesh=mesh, in_specs=in_specs, out_specs=out_specs, check_vma=False)
```

```python
import functools
import math

import jax
import jax.numpy as jnp
import ml_dtypes
import numpy as np
from jax import lax
from jax.experimental import pallas as pl
from jax.experimental.pallas import tpu as pltpu
from jax.sharding import PartitionSpec as P

MESH = pl.DeviceIdType.MESH
F32, BF16 = jnp.float32, jnp.bfloat16

N = 16
ROWS = 12
WIDTH = 64
NLAT = N * ROWS
NLON = 768
Q = 3
GROUPS = 3
PART = 48
OFFSETS = sorted(
    (divmod(s, 4) for s in range(1, N)), key=lambda o: -min(o[0], 4 - o[0]) - min(o[1], 4 - o[1])
)


@functools.lru_cache(None)
def constants():
    f32, bf16 = np.float32, ml_dtypes.bfloat16
    orders = np.arange(NLAT)
    angle = 2.0 * np.pi / NLON * (orders[:, None] * np.arange(NLON)[None, :] % NLON)
    parts = np.concatenate([np.cos(angle), -np.sin(angle)], axis=0)
    factor = np.where(orders == 0, 1.0, 2.0)[:, None]
    forward = (2.0 * np.pi / NLON * parts).astype(bf16)
    inverse = (np.concatenate([factor, factor], axis=0) * parts).astype(bf16)

    theta = np.pi * (np.arange(NLAT) + 0.5) / NLAT
    cosine, sine = np.cos(theta), np.sin(theta)
    weights = np.pi / NLAT * sine
    row_weights = np.zeros((N, 16, 128), f32)
    row_weights[:, :ROWS] = weights.reshape(N, ROWS, 1)

    lane = np.arange(256)
    s, i, r = lane // 16, lane % 16 // 4, lane % 4
    rows_of = [ROWS * s + 4 * q + r for q in range(Q)]
    col_weights = np.stack([np.repeat(weights[j][:, None], 128, 1) for j in rows_of]).astype(f32)

    diagonal = np.zeros((NLAT, NLAT))
    diagonal[0] = 1.0 / math.sqrt(4.0 * math.pi)
    for m in range(1, NLAT):
        diagonal[m] = -math.sqrt((2.0 * m + 1.0) / (2.0 * m)) * sine * diagonal[m - 1]
    m, l = np.arange(NLAT)[:, None].astype(float), np.arange(NLAT)[None, :].astype(float)
    above = l > m
    scale = np.sqrt(np.where(above, 4 * l * l - 1, 0.0) / np.where(above, l * l - m * m, 1.0))
    last = l - 1
    two = last > m
    scale_last = np.sqrt(np.where(two, 4 * last * last - 1, 1.0) / np.where(two, last * last - m * m, 1.0))
    back = np.where(two, scale / scale_last, 0.0)

    cos_map = np.zeros((16, 256), f32)
    order_map = np.full((16, 256), -1.0, f32)
    diag_map = np.zeros((N, 16, 256), f32)
    coef = np.zeros((N, 64, 256), f32)
    for q in range(Q):
        for g in range(GROUPS):
            cos_map[4 * q + g] = cosine[rows_of[q]]
            order_map[4 * q + g] = 4 * g + i
            for d in range(N):
                diag_map[d, 4 * q + g] = diagonal[ROWS * d + 4 * g + i, rows_of[q]]
    for g in range(GROUPS):
        for k in range(4):
            for d in range(N):
                for kind, values in enumerate((scale, back)):
                    for copy in range(2):
                        coef[d, 32 * kind + 8 * k + 4 * copy + g, :NLAT] = values[ROWS * d + 4 * g + k]
    maps = np.concatenate([cos_map, order_map], axis=0)
    return dict(
        forward=forward, inverse=inverse, row_weights=row_weights, col_weights=col_weights,
        maps=maps, diag=diag_map, coef=coef,
    )


def kernel(
    x_hbm, cot_hbm, weight_hbm, ft_hbm, gt_hbm, roww_hbm, colw_hbm, maps_hbm, diag_hbm, coef_hbm,
    act_hbm, gf_hbm, gw_hbm,
    xv, cotv, weightv, ftv, gtv, rowwv, colwv, mapsv, diagv, coefv,
    stage, send, recv, legendre0, legendre1, table, table_t, coeffs, dcoeffs, filtered, rotated, prev, tt, actv,
    dprev, gsend, grecv, gout, gall, sums, gwv,
    load_sem, store_sem, send_a, recv_a, send_r, recv_r,
):
    dp, me = lax.axis_index("dp"), lax.axis_index("spatial")
    mx, my = me // 4, lax.rem(me, 4)
    at = lambda dx, dy: lax.rem(mx + dx, 4) * 4 + lax.rem(my + dy, 4)
    peer_of = lambda s: lax.rem(me + s, N)

    def each_peer(action):
        def one(s, _):
            action(peer_of(s))
            return 0

        lax.fori_loop(1, N, one, 0)

    barrier = pltpu.get_barrier_semaphore()
    for dx, dy in OFFSETS:
        pl.semaphore_signal(barrier, inc=1, device_id=(dp, at(dx, dy)), device_id_type=MESH)

    quad = lambda q: pl.ds(pl.multiple_of(q * 256, 256), 256)

    def x_load(q):
        return pltpu.make_async_copy(x_hbm.at[quad(q)], xv.at[quad(q)], load_sem.at[q])

    loads = [
        pltpu.make_async_copy(src, dst, load_sem.at[3 + i])
        for i, (src, dst) in enumerate((
            (ft_hbm, ftv), (roww_hbm.at[me], rowwv), (coef_hbm.at[me], coefv),
            (diag_hbm.at[me], diagv), (maps_hbm, mapsv), (weight_hbm, weightv), (gt_hbm, gtv),
            (cot_hbm, cotv), (colw_hbm, colwv),
        ))
    ]
    loads[0].start()
    x_load(0).start()
    loads[1].start()
    x_load(1).start()
    x_load(2).start()
    for load in loads[2:]:
        load.start()

    low = lax.broadcasted_iota(jnp.int32, (1, 128), 1) < WIDTH
    half = lambda value: pltpu.roll(value, WIDTH, 1)

    def outgoing(phase, q, peer):
        return pltpu.make_async_remote_copy(
            src_ref=send.at[phase, q, peer], dst_ref=recv.at[phase, q, me],
            send_sem=send_a.at[phase, q, peer], recv_sem=recv_a.at[phase, q, me],
            device_id=(dp, peer), device_id_type=MESH,
        )

    def arrivals(phase, q):
        def arrival(src):
            ref = recv.at[phase, q, src]
            pltpu.make_async_remote_copy(
                src_ref=ref, dst_ref=ref, send_sem=send_a.at[phase, q, src], recv_sem=recv_a.at[phase, q, src],
                device_id=(dp, src), device_id_type=MESH,
            ).wait_recv()

        each_peer(arrival)

    def ship(phase, q):
        for dx, dy in OFFSETS:
            outgoing(phase, q, at(dx, dy)).start()
        recv[phase, q, me] = send[phase, q, me]

    def fourier(phase, q, rows_ref, factors, scaled):
        block = rows_ref[quad(q), :]
        out = lax.dot_general(factors[...], block, (((1,), (1,)), ((), ())), preferred_element_type=F32)
        for u in range(2):
            real, imag = out[:NLAT, 128 * u : 128 * u + 128], out[NLAT:, 128 * u : 128 * u + 128]
            pair = (jnp.where(low, real, half(imag)), jnp.where(low, half(real), imag))
            for i, value in enumerate(pair):
                r = 2 * u + i
                if scaled:
                    value = value * rowwv[pl.ds(4 * q + r, 1), :]
                stage[pl.ds(r, NLAT, stride=4), :] = value
        send[phase, q] = stage[...].astype(BF16).reshape(N, PART, 128)

    loads[0].wait()
    loads[1].wait()
    x_load(0).wait()
    fourier(0, 0, xv, ftv, True)
    pl.semaphore_wait(barrier, N - 1)
    ship(0, 0)

    def spectra(q, _):
        x_load(q).wait()
        fourier(0, q, xv, ftv, True)
        ship(0, q)
        return 0

    lax.fori_loop(1, Q, spectra, 0)

    for load in loads[2:]:
        load.wait()
    order_of_lane = lax.broadcasted_iota(jnp.int32, (1, 128), 1) % 16 // 4
    first = (ROWS * me).astype(F32)

    for h in range(2):
        def degrees(g, carry, h=h):
            turned = pltpu.roll(coefv[:, 128 * h : 128 * h + 128], lax.rem(128 - 8 * g, 128), 1)
            for i in range(8):
                l = 128 * h + 8 * g + i
                pick = lambda k: jnp.broadcast_to(turned[8 * k : 8 * k + 8, i : i + 1], (8, 128))
                choose = lambda k: jnp.where(
                    order_of_lane < 2,
                    jnp.where(order_of_lane == 0, pick(k), pick(k + 1)),
                    jnp.where(order_of_lane == 2, pick(k + 2), pick(k + 3)),
                )
                scale, back = choose(0), choose(4)
                scale, back = jnp.concatenate([scale, scale], axis=0), jnp.concatenate([back, back], axis=0)
                new = []
                for u, store in ((0, legendre0), (1, legendre1)):
                    cols = slice(128 * u, 128 * u + 128)
                    last, before = carry[2 * u], carry[2 * u + 1]
                    start = jnp.where(mapsv[16:, cols] + first == l.astype(F32), diagv[:, cols], 0.0)
                    value = (scale * mapsv[:16, cols]) * last + (start - back * before)
                    store[pl.ds(l, 16, stride=NLAT), :] = value
                    new += [value, last]
                carry = tuple(new)
            return carry

        if h == 0:
            carry = (jnp.zeros((16, 128), F32),) * 4
        carry = lax.fori_loop(0, 16 if h == 0 else 8, degrees, carry)

    def finish(v, _):
        rows = pl.ds(pl.multiple_of((4 * (v // GROUPS) + lax.rem(v, GROUPS)) * NLAT, NLAT), NLAT)
        for u, store in ((0, legendre0), (1, legendre1)):
            part = store[rows, :].astype(BF16)
            table[v, :, 128 * u : 128 * u + 128] = part
            table_t[v, 128 * u : 128 * u + 128, :] = part.T
        return 0

    lax.fori_loop(0, Q * GROUPS, finish, 0)

    weights = weightv[...].T
    rotated[0] = jnp.where(low, weights, half(weights))
    rotated[1] = jnp.where(low, -half(weights), weights)
    coeffs[...] = jnp.zeros_like(coeffs)
    dcoeffs[...] = jnp.zeros_like(dcoeffs)
    sums[...] = jnp.zeros_like(sums)

    order_of_row = lax.broadcasted_iota(jnp.int32, (256, 128), 0) % 16 // 4
    upper = lax.broadcasted_iota(jnp.int32, (1, 8, 128), 1) < 4
    tile = lambda g: pl.ds(pl.multiple_of(g * 16, 16), 16)

    def analyse(phase, q, into):
        arrivals(phase, q)

        def one(g, _):
            block = recv[phase, q, :, tile(g), :].reshape(256, 128)
            zero = jnp.zeros_like(block)
            spread = jnp.concatenate([jnp.where(order_of_row == k, block, zero) for k in range(4)], axis=1)
            into[g] = into[g] + jnp.dot(table[GROUPS * q + g], spread, preferred_element_type=F32)
            return 0

        lax.fori_loop(0, GROUPS, one, 0)
        return 0

    def synthesize(phase, q, scaled):
        def one(g, _):
            out = jnp.dot(table_t[GROUPS * q + g], filtered[g], preferred_element_type=F32)
            parts = [out[:, 128 * k : 128 * k + 128].reshape(N, 2, 8, 128) for k in range(4)]
            first_half = jnp.where(upper, parts[0][:, 0], parts[1][:, 0])
            second_half = jnp.where(upper, parts[2][:, 1], parts[3][:, 1])
            out = jnp.concatenate([first_half, second_half], axis=1)
            if scaled:
                out = out * colwv[q].reshape(N, 16, 128)
            send[phase, q, :, tile(g), :] = out.astype(BF16)
            return 0

        lax.fori_loop(0, GROUPS, one, 0)
        ship(phase, q)
        return 0

    lax.fori_loop(0, Q, lambda q, _: analyse(0, q, coeffs), 0)

    def filter_group(g, _):
        for k in range(4):
            cols = slice(128 * k, 128 * k + 128)
            value = coeffs[g, :, cols]
            filtered[g, :, cols] = (rotated[0] * value + rotated[1] * half(value)).astype(BF16)
        return 0

    lax.fori_loop(0, GROUPS, filter_group, 0)
    lax.fori_loop(0, Q, lambda q, _: synthesize(1, q, False), 0)

    def gather(phase, q):
        arrivals(phase, q)
        stage[...] = recv[phase, q].reshape(N * PART, 128).astype(F32)
        for r in range(4):
            turned = stage[pl.ds(r, NLAT, stride=4), :].astype(BF16).T
            tt[0, WIDTH * r : WIDTH * r + WIDTH, :] = turned[:WIDTH]
            tt[1, WIDTH * r : WIDTH * r + WIDTH, :] = turned[WIDTH:]

    def grid_rows(factors):
        return jnp.dot(tt[0], factors[:NLAT, :], preferred_element_type=F32) + jnp.dot(
            tt[1], factors[NLAT:, :], preferred_element_type=F32
        )

    def act_store(q):
        return pltpu.make_async_copy(actv.at[quad(q)], act_hbm.at[quad(q)], store_sem.at[q])

    def activation(q, _):
        gather(1, q)
        prev[...] = grid_rows(gtv)

        def strip(i, _):
            here = pl.ds(pl.multiple_of(i * 16, 16), 16)
            there = pl.ds(pl.multiple_of(q * 256 + i * 16, 16), 16)
            pre = prev[here, :]
            cdf = 0.5 + 0.5 * lax.erf(pre * (1.0 / math.sqrt(2.0)))
            density = jnp.exp(-0.5 * pre * pre) * (1.0 / math.sqrt(2.0 * math.pi))
            actv[there, :] = (pre * cdf).astype(BF16)
            dprev[there, :] = (cotv[there, :].astype(F32) * (cdf + pre * density)).astype(BF16)
            return 0

        lax.fori_loop(0, 16, strip, 0)
        fourier(2, q, dprev, gtv, False)
        ship(2, q)
        act_store(q).start()
        return 0

    lax.fori_loop(0, Q, activation, 0)

    lax.fori_loop(0, Q, lambda q, _: analyse(2, q, dcoeffs), 0)

    def adjoint_group(g, _):
        for k in range(4):
            cols = slice(128 * k, 128 * k + 128)
            value = dcoeffs[g, :, cols]
            filtered[g, :, cols] = (rotated[0] * value - rotated[1] * half(value)).astype(BF16)
        return 0

    lax.fori_loop(0, GROUPS, adjoint_group, 0)
    synthesize(3, 0, True)

    def sum_group(g, _):
        for k in range(4):
            cols = slice(128 * k, 128 * k + 128)
            value, coeff = dcoeffs[g, :, cols], coeffs[g, :, cols]
            sums[0] = sums[0] + value * coeff
            sums[1] = sums[1] + value * half(coeff)
        return 0

    lax.fori_loop(0, GROUPS, sum_group, 0)
    same, cross = sums[0], sums[1]
    partial = jnp.where(low, same + half(same), cross - half(cross)).astype(BF16)
    gsend[:ROWS] = partial.reshape(ROWS, 16, 128)
    gsend[ROWS:] = jnp.zeros((N - ROWS, 16, 128), BF16)

    def small_copy(turn, peer):
        return pltpu.make_async_remote_copy(
            src_ref=gout if turn else gsend.at[peer], dst_ref=(gall if turn else grecv).at[me],
            send_sem=send_r.at[turn, peer], recv_sem=recv_r.at[turn, me],
            device_id=(dp, peer), device_id_type=MESH,
        )

    def small_arrivals(turn):
        def arrival(src):
            ref = (gall if turn else grecv).at[src]
            pltpu.make_async_remote_copy(
                src_ref=ref, dst_ref=ref, send_sem=send_r.at[turn, src], recv_sem=recv_r.at[turn, src],
                device_id=(dp, src), device_id_type=MESH,
            ).wait_recv()

        each_peer(arrival)

    each_peer(lambda peer: small_copy(0, peer).start())
    grecv[me] = gsend[me]
    lax.fori_loop(1, Q, lambda q, _: synthesize(3, q, True), 0)

    small_arrivals(0)
    total = (jnp.sum(grecv[...].astype(F32), axis=0) * (1.0 / NLAT)).astype(BF16)
    gout[...] = total
    gall[me] = total
    each_peer(lambda peer: small_copy(1, peer).start())

    def gf_store(q):
        return pltpu.make_async_copy(xv.at[quad(q)], gf_hbm.at[quad(q)], store_sem.at[3 + q])

    def gradient(q, _):
        gather(3, q)
        xv[quad(q), :] = grid_rows(ftv).astype(BF16)
        gf_store(q).start()
        return 0

    lax.fori_loop(0, Q, gradient, 0)

    small_arrivals(1)
    gwv[...] = gall[:ROWS].reshape(NLAT, 128).astype(F32).T
    gw_store = pltpu.make_async_copy(gwv, gw_hbm, store_sem.at[6])
    gw_store.start()

    def drain(s, _):
        peer = peer_of(s)
        for phase in range(4):
            for q in range(Q):
                outgoing(phase, q, peer).wait_send()
        for turn in range(2):
            small_copy(turn, peer).wait_send()
        return 0

    lax.fori_loop(1, N, drain, 0)
    for q in range(Q):
        act_store(q).wait()
        gf_store(q).wait()
    gw_store.wait()


def hand_over(*refs):
    count = (len(refs) - 1) // 2
    copies = [pltpu.make_async_copy(refs[i], refs[count + i], refs[-1].at[i]) for i in range(count)]
    for copy in copies:
        copy.start()
    for copy in copies:
        copy.wait()


def shards(fields, filter_weight, cotangent):
    rows, width, nlon = fields.shape
    if (rows, width, nlon) != (ROWS, WIDTH, NLON) or lax.axis_size("spatial") != N:
        raise ValueError("unexpected sizes")
    held = constants()
    names = ("forward", "inverse", "row_weights", "col_weights", "maps", "diag", "coef")
    flat = rows * width
    dma, vmem = pltpu.SemaphoreType.DMA, pltpu.VMEM
    shapes = (
        jax.ShapeDtypeStruct((flat, nlon), BF16),
        jax.ShapeDtypeStruct((flat, nlon), BF16),
        jax.ShapeDtypeStruct((2 * width, NLAT), F32),
    )
    results = pl.pallas_call(
        kernel,
        out_shape=shapes,
        in_specs=[pl.BlockSpec(memory_space=pl.ANY)] * 10,
        out_specs=(pl.BlockSpec(memory_space=pl.ANY),) * 3,
        scratch_shapes=[
            vmem((flat, nlon), BF16), vmem((flat, nlon), BF16), vmem((2 * width, NLAT), F32),
            vmem((2 * NLAT, nlon), BF16), vmem((2 * NLAT, nlon), BF16), vmem((16, 128), F32),
            vmem((Q, 256, 128), F32), vmem((32, 256), F32), vmem((16, 256), F32), vmem((64, 256), F32),
            vmem((N * PART, 128), F32), vmem((4, Q, N, PART, 128), BF16), vmem((4, Q, N, PART, 128), BF16),
            vmem((16 * NLAT, 128), F32), vmem((16 * NLAT, 128), F32),
            vmem((Q * GROUPS, NLAT, 256), BF16), vmem((Q * GROUPS, 256, NLAT), BF16),
            vmem((GROUPS, NLAT, 512), F32), vmem((GROUPS, NLAT, 512), F32), vmem((GROUPS, NLAT, 512), BF16),
            vmem((2, NLAT, 128), F32), vmem((256, nlon), F32),
            vmem((2, 256, NLAT), BF16), vmem((flat, nlon), BF16), vmem((flat, nlon), BF16),
            vmem((N, 16, 128), BF16), vmem((N, 16, 128), BF16), vmem((16, 128), BF16), vmem((N, 16, 128), BF16),
            vmem((2, NLAT, 128), F32), vmem((2 * width, NLAT), F32),
            dma((12,)), dma((7,)), dma((4, Q, N)), dma((4, Q, N)), dma((2, N)), dma((2, N)),
        ],
        compiler_params=pltpu.CompilerParams(
            collective_id=0, has_side_effects=True, vmem_limit_bytes=56 << 20
        ),
    )(
        fields.reshape(flat, nlon), cotangent.reshape(flat, nlon), filter_weight.reshape(2 * width, NLAT),
        *(jnp.asarray(held[name]) for name in names),
    )
    activated, grad_fields, grad_weight = pl.pallas_call(
        hand_over,
        out_shape=shapes,
        in_specs=[pl.BlockSpec(memory_space=pl.ANY)] * 3,
        out_specs=(pl.BlockSpec(memory_space=pl.ANY),) * 3,
        scratch_shapes=[dma((3,))],
    )(*results)
    return (
        activated.reshape(rows, width, nlon), grad_fields.reshape(rows, width, nlon),
        grad_weight.reshape(2, width, NLAT),
    )


def solution(mesh):
    in_specs = (P("spatial", "dp", None), P(None, "dp", None), P("spatial", "dp", None))
    out_specs = (P("spatial", "dp", None), P("spatial", "dp", None), P(None, "dp", None))
    return jax.shard_map(shards, mesh=mesh, in_specs=in_specs, out_specs=out_specs, check_vma=False)
```

```python
import functools
import math

import jax
import jax.numpy as jnp
import ml_dtypes
import numpy as np
from jax import lax
from jax.experimental import pallas as pl
from jax.experimental.pallas import tpu as pltpu
from jax.sharding import PartitionSpec as P

MESH = pl.DeviceIdType.MESH
F32, BF16 = jnp.float32, jnp.bfloat16

N = 16
ROWS = 12
WIDTH = 64
NLAT = N * ROWS
NLON = 768
Q = 3
GROUPS = 3
PART = 48
OFFSETS = sorted(
    (divmod(s, 4) for s in range(1, N)), key=lambda o: -min(o[0], 4 - o[0]) - min(o[1], 4 - o[1])
)


@functools.lru_cache(None)
def constants():
    f32, bf16 = np.float32, ml_dtypes.bfloat16
    orders = np.arange(NLAT)
    angle = 2.0 * np.pi / NLON * (orders[:, None] * np.arange(NLON)[None, :] % NLON)
    parts = np.concatenate([np.cos(angle), -np.sin(angle)], axis=0)
    factor = np.where(orders == 0, 1.0, 2.0)[:, None]
    forward = (2.0 * np.pi / NLON * parts).astype(bf16)
    inverse = (np.concatenate([factor, factor], axis=0) * parts).astype(bf16)

    theta = np.pi * (np.arange(NLAT) + 0.5) / NLAT
    cosine, sine = np.cos(theta), np.sin(theta)
    weights = np.pi / NLAT * sine
    row_weights = np.zeros((N, 16, 128), f32)
    row_weights[:, :ROWS] = weights.reshape(N, ROWS, 1)

    lane = np.arange(256)
    s, i, r = lane // 16, lane % 16 // 4, lane % 4
    rows_of = [ROWS * s + 4 * q + r for q in range(Q)]
    col_weights = np.stack([np.repeat(weights[j][:, None], 128, 1) for j in rows_of]).astype(f32)

    diagonal = np.zeros((NLAT, NLAT))
    diagonal[0] = 1.0 / math.sqrt(4.0 * math.pi)
    for m in range(1, NLAT):
        diagonal[m] = -math.sqrt((2.0 * m + 1.0) / (2.0 * m)) * sine * diagonal[m - 1]
    m, l = np.arange(NLAT)[:, None].astype(float), np.arange(NLAT)[None, :].astype(float)
    above = l > m
    scale = np.sqrt(np.where(above, 4 * l * l - 1, 0.0) / np.where(above, l * l - m * m, 1.0))
    last = l - 1
    two = last > m
    scale_last = np.sqrt(np.where(two, 4 * last * last - 1, 1.0) / np.where(two, last * last - m * m, 1.0))
    back = np.where(two, scale / scale_last, 0.0)

    cos_map = np.zeros((16, 256), f32)
    order_map = np.full((16, 256), -1.0, f32)
    diag_map = np.zeros((N, 16, 256), f32)
    coef = np.zeros((N, 64, 256), f32)
    for q in range(Q):
        for g in range(GROUPS):
            cos_map[4 * q + g] = cosine[rows_of[q]]
            order_map[4 * q + g] = 4 * g + i
            for d in range(N):
                diag_map[d, 4 * q + g] = diagonal[ROWS * d + 4 * g + i, rows_of[q]]
    for g in range(GROUPS):
        for k in range(4):
            for d in range(N):
                for kind, values in enumerate((scale, back)):
                    for copy in range(2):
                        coef[d, 32 * kind + 8 * k + 4 * copy + g, :NLAT] = values[ROWS * d + 4 * g + k]
    maps = np.concatenate([cos_map, order_map], axis=0)
    return dict(
        forward=forward, inverse=inverse, row_weights=row_weights, col_weights=col_weights,
        maps=maps, diag=diag_map, coef=coef,
    )


def kernel(
    x_hbm, cot_hbm, weight_hbm, ft_hbm, gt_hbm, roww_hbm, colw_hbm, maps_hbm, diag_hbm, coef_hbm,
    act_hbm, gf_hbm, gw_hbm,
    xv, cotv, weightv, ftv, gtv, rowwv, colwv, mapsv, diagv, coefv,
    stage, send, recv, legendre0, legendre1, table, table_t, coeffs, dcoeffs, filtered, rotated, prev, tt, actv,
    dprev, gsend, grecv, gout, gall, sums, gwv,
    load_sem, store_sem, send_a, recv_a, send_r, recv_r,
):
    dp, me = lax.axis_index("dp"), lax.axis_index("spatial")
    mx, my = me // 4, lax.rem(me, 4)
    at = lambda dx, dy: lax.rem(mx + dx, 4) * 4 + lax.rem(my + dy, 4)
    peer_of = lambda s: lax.rem(me + s, N)

    def each_peer(action):
        def one(s, _):
            action(peer_of(s))
            return 0

        lax.fori_loop(1, N, one, 0)

    barrier = pltpu.get_barrier_semaphore()
    for dx, dy in OFFSETS:
        pl.semaphore_signal(barrier, inc=1, device_id=(dp, at(dx, dy)), device_id_type=MESH)

    quad = lambda q: pl.ds(pl.multiple_of(q * 256, 256), 256)

    def x_load(q):
        return pltpu.make_async_copy(x_hbm.at[quad(q)], xv.at[quad(q)], load_sem.at[q])

    loads = [
        pltpu.make_async_copy(src, dst, load_sem.at[3 + i])
        for i, (src, dst) in enumerate((
            (ft_hbm, ftv), (roww_hbm.at[me], rowwv), (coef_hbm.at[me], coefv),
            (diag_hbm.at[me], diagv), (maps_hbm, mapsv), (weight_hbm, weightv), (gt_hbm, gtv),
            (cot_hbm, cotv), (colw_hbm, colwv),
        ))
    ]
    loads[0].start()
    x_load(0).start()
    loads[1].start()
    x_load(1).start()
    x_load(2).start()
    for load in loads[2:5]:
        load.start()

    low = lax.broadcasted_iota(jnp.int32, (1, 128), 1) < WIDTH
    half = lambda value: pltpu.roll(value, WIDTH, 1)

    def outgoing(phase, q, peer):
        return pltpu.make_async_remote_copy(
            src_ref=send.at[phase, q, peer], dst_ref=recv.at[phase, q, me],
            send_sem=send_a.at[phase, q], recv_sem=recv_a.at[phase, q],
            device_id=(dp, peer), device_id_type=MESH,
        )

    def whole(phase, q):
        return pltpu.make_async_remote_copy(
            src_ref=send.at[phase, q, pl.ds(0, N - 1)], dst_ref=recv.at[phase, q, pl.ds(0, N - 1)],
            send_sem=send_a.at[phase, q], recv_sem=recv_a.at[phase, q],
            device_id=(dp, peer_of(1)), device_id_type=MESH,
        )

    def ship(phase, q):
        for dx, dy in OFFSETS:
            outgoing(phase, q, at(dx, dy)).start()
        recv[phase, q, me] = send[phase, q, me]

    def fourier(phase, q, rows_ref, factors, scaled):
        block = rows_ref[quad(q), :]
        out = lax.dot_general(factors[...], block, (((1,), (1,)), ((), ())), preferred_element_type=F32)
        for u in range(2):
            real, imag = out[:NLAT, 128 * u : 128 * u + 128], out[NLAT:, 128 * u : 128 * u + 128]
            pair = (jnp.where(low, real, half(imag)), jnp.where(low, half(real), imag))
            for i, value in enumerate(pair):
                r = 2 * u + i
                if scaled:
                    value = value * rowwv[pl.ds(4 * q + r, 1), :]
                stage[pl.ds(r, NLAT, stride=4), :] = value
        send[phase, q] = stage[...].astype(BF16).reshape(N, PART, 128)

    loads[0].wait()
    loads[1].wait()
    x_load(0).wait()
    fourier(0, 0, xv, ftv, True)
    pl.semaphore_wait(barrier, N - 1)
    ship(0, 0)
    for load in loads[5:]:
        load.start()

    def spectra(q, _):
        x_load(q).wait()
        fourier(0, q, xv, ftv, True)
        ship(0, q)
        return 0

    lax.fori_loop(1, Q, spectra, 0)

    for load in loads[2:5]:
        load.wait()
    order_of_lane = lax.broadcasted_iota(jnp.int32, (1, 128), 1) % 16 // 4
    first = (ROWS * me).astype(F32)

    for h in range(2):
        def degrees(g, carry, h=h):
            turned = pltpu.roll(coefv[:, 128 * h : 128 * h + 128], lax.rem(128 - 32 * g, 128), 1)
            for i in range(32):
                l = 128 * h + 32 * g + i
                pick = lambda k: jnp.broadcast_to(turned[8 * k : 8 * k + 8, i : i + 1], (8, 128))
                choose = lambda k: jnp.where(
                    order_of_lane < 2,
                    jnp.where(order_of_lane == 0, pick(k), pick(k + 1)),
                    jnp.where(order_of_lane == 2, pick(k + 2), pick(k + 3)),
                )
                scale, back = choose(0), choose(4)
                scale, back = jnp.concatenate([scale, scale], axis=0), jnp.concatenate([back, back], axis=0)
                new = []
                for u, store in ((0, legendre0), (1, legendre1)):
                    cols = slice(128 * u, 128 * u + 128)
                    last, before = carry[2 * u], carry[2 * u + 1]
                    start = jnp.where(mapsv[16:, cols] + first == l.astype(F32), diagv[:, cols], 0.0)
                    value = (scale * mapsv[:16, cols]) * last + (start - back * before)
                    store[pl.ds(l, 16, stride=NLAT), :] = value
                    new += [value, last]
                carry = tuple(new)
            return carry

        if h == 0:
            carry = (jnp.zeros((16, 128), F32),) * 4
        carry = lax.fori_loop(0, 4 if h == 0 else 2, degrees, carry)

    def finish(v, _):
        rows = pl.ds(pl.multiple_of((4 * (v // GROUPS) + lax.rem(v, GROUPS)) * NLAT, NLAT), NLAT)
        for u, store in ((0, legendre0), (1, legendre1)):
            part = store[rows, :].astype(BF16)
            table[v, :, 128 * u : 128 * u + 128] = part
        return 0

    lax.fori_loop(0, Q * GROUPS, finish, 0)

    for load in loads[5:]:
        load.wait()
    weights = weightv[...].T
    rotated[0] = jnp.where(low, weights, half(weights))
    rotated[1] = jnp.where(low, -half(weights), weights)
    coeffs[...] = jnp.zeros_like(coeffs)
    dcoeffs[...] = jnp.zeros_like(dcoeffs)
    sums[...] = jnp.zeros_like(sums)

    order_of_row = lax.broadcasted_iota(jnp.int32, (256, 128), 0) % 16 // 4
    upper = lax.broadcasted_iota(jnp.int32, (1, 8, 128), 1) < 4
    tile = lambda g: pl.ds(g * 16, 16)

    def analyse(phase, q, into):
        whole(phase, q).wait_recv()

        def one(g, _):
            block = recv[phase, q, :, tile(g), :].reshape(256, 128)
            zero = jnp.zeros_like(block)
            spread = jnp.concatenate([jnp.where(order_of_row == k, block, zero) for k in range(4)], axis=1)
            into[g] = into[g] + jnp.dot(table[GROUPS * q + g], spread, preferred_element_type=F32)
            return 0

        for g in range(GROUPS):
            one(g, 0)
        return 0

    def synthesize(phase, q, scaled):
        def one(g, _):
            out = jnp.dot(table_t[GROUPS * q + g], filtered[g], preferred_element_type=F32)
            parts = [out[:, 128 * k : 128 * k + 128].reshape(N, 2, 8, 128) for k in range(4)]
            first_half = jnp.where(upper, parts[0][:, 0], parts[1][:, 0])
            second_half = jnp.where(upper, parts[2][:, 1], parts[3][:, 1])
            out = jnp.concatenate([first_half, second_half], axis=1)
            if scaled:
                out = out * colwv[q].reshape(N, 16, 128)
            send[phase, q, :, tile(g), :] = out.astype(BF16)
            return 0

        for g in range(GROUPS):
            one(g, 0)
        ship(phase, q)
        return 0

    def turn_table(v, _):
        table_t[v] = table[v].T
        return 0

    def forward_chunk(q, _):
        analyse(0, q, coeffs)

        @pl.when(q == 1)
        def _():
            lax.fori_loop(0, Q * GROUPS, turn_table, 0)

        return 0

    lax.fori_loop(0, Q, forward_chunk, 0)

    def filter_group(g, _):
        for k in range(4):
            cols = slice(128 * k, 128 * k + 128)
            value = coeffs[g, :, cols]
            filtered[g, :, cols] = (rotated[0] * value + rotated[1] * half(value)).astype(BF16)
        return 0

    for g in range(GROUPS):
        filter_group(g, 0)
    lax.fori_loop(0, Q, lambda q, _: synthesize(1, q, False), 0)

    def gather(phase, q):
        whole(phase, q).wait_recv()
        stage[...] = recv[phase, q].reshape(N * PART, 128).astype(F32)
        for r in range(4):
            turned = stage[pl.ds(r, NLAT, stride=4), :].astype(BF16).T
            tt[0, WIDTH * r : WIDTH * r + WIDTH, :] = turned[:WIDTH]
            tt[1, WIDTH * r : WIDTH * r + WIDTH, :] = turned[WIDTH:]

    def grid_rows(factors):
        return jnp.dot(tt[0], factors[:NLAT, :], preferred_element_type=F32) + jnp.dot(
            tt[1], factors[NLAT:, :], preferred_element_type=F32
        )

    def act_store(q):
        return pltpu.make_async_copy(actv.at[quad(q)], act_hbm.at[quad(q)], store_sem.at[q])

    def activation(q, _):
        gather(1, q)
        prev[...] = grid_rows(gtv)

        def strip(i, _):
            here = pl.ds(pl.multiple_of(i * 16, 16), 16)
            there = pl.ds(pl.multiple_of(q * 256 + i * 16, 16), 16)
            pre = prev[here, :]
            cdf = 0.5 + 0.5 * lax.erf(pre * (1.0 / math.sqrt(2.0)))
            density = jnp.exp(-0.5 * pre * pre) * (1.0 / math.sqrt(2.0 * math.pi))
            actv[there, :] = (pre * cdf).astype(BF16)
            dprev[there, :] = (cotv[there, :].astype(F32) * (cdf + pre * density)).astype(BF16)
            return 0

        lax.fori_loop(0, 16, strip, 0)
        fourier(2, q, dprev, gtv, False)
        ship(2, q)
        act_store(q).start()
        return 0

    lax.fori_loop(0, Q, activation, 0)

    lax.fori_loop(0, Q, lambda q, _: analyse(2, q, dcoeffs), 0)

    def adjoint_group(g, _):
        for k in range(4):
            cols = slice(128 * k, 128 * k + 128)
            value = dcoeffs[g, :, cols]
            filtered[g, :, cols] = (rotated[0] * value - rotated[1] * half(value)).astype(BF16)
        return 0

    for g in range(GROUPS):
        adjoint_group(g, 0)
    synthesize(3, 0, True)

    def sum_group(g, _):
        for k in range(4):
            cols = slice(128 * k, 128 * k + 128)
            value, coeff = dcoeffs[g, :, cols], coeffs[g, :, cols]
            sums[0] = sums[0] + value * coeff
            sums[1] = sums[1] + value * half(coeff)
        return 0

    lax.fori_loop(0, GROUPS, sum_group, 0)
    same, cross = sums[0], sums[1]
    partial = jnp.where(low, same + half(same), cross - half(cross)).astype(BF16)
    gsend[:ROWS] = partial.reshape(ROWS, 16, 128)
    gsend[ROWS:] = jnp.zeros((N - ROWS, 16, 128), BF16)

    def small_copy(turn, peer):
        return pltpu.make_async_remote_copy(
            src_ref=gout if turn else gsend.at[peer], dst_ref=(gall if turn else grecv).at[me],
            send_sem=send_r.at[turn], recv_sem=recv_r.at[turn],
            device_id=(dp, peer), device_id_type=MESH,
        )

    def small_whole(turn):
        ref = (gall if turn else grecv).at[pl.ds(0, N - 1)]
        return pltpu.make_async_remote_copy(
            src_ref=gsend.at[pl.ds(0, N - 1)], dst_ref=ref, send_sem=send_r.at[turn], recv_sem=recv_r.at[turn],
            device_id=(dp, peer_of(1)), device_id_type=MESH,
        )

    each_peer(lambda peer: small_copy(0, peer).start())
    grecv[me] = gsend[me]
    synthesize(3, 1, True)
    small_whole(0).wait_recv()
    total = (jnp.sum(grecv[...].astype(F32), axis=0) * (1.0 / NLAT)).astype(BF16)
    gout[...] = total
    gall[me] = total
    each_peer(lambda peer: small_copy(1, peer).start())
    synthesize(3, 2, True)

    def gf_store(q):
        return pltpu.make_async_copy(xv.at[quad(q)], gf_hbm.at[quad(q)], store_sem.at[3 + q])

    def gradient(q, _):
        gather(3, q)
        xv[quad(q), :] = grid_rows(ftv).astype(BF16)
        gf_store(q).start()
        return 0

    lax.fori_loop(0, Q, gradient, 0)

    small_whole(1).wait_recv()
    gwv[...] = gall[:ROWS].reshape(NLAT, 128).astype(F32).T
    gw_store = pltpu.make_async_copy(gwv, gw_hbm, store_sem.at[6])
    gw_store.start()

    for phase in range(4):
        for q in range(Q):
            whole(phase, q).wait_send()
    for turn in range(2):
        small_whole(turn).wait_send()
    for q in range(Q):
        act_store(q).wait()
        gf_store(q).wait()
    gw_store.wait()


def hand_over(act, gf, gw, act_out, gf_out, gw_out, act_v, gf_v, gw_v, sems):
    moves = [(gw, gw_v, gw_out)]
    for q in range(Q):
        rows = pl.ds(256 * q, 256)
        moves += [(src.at[rows], mid.at[rows], dst.at[rows]) for src, mid, dst in ((act, act_v, act_out), (gf, gf_v, gf_out))]
    ins = [pltpu.make_async_copy(src, mid, sems.at[0, i]) for i, (src, mid, _) in enumerate(moves)]
    outs = [pltpu.make_async_copy(mid, dst, sems.at[1, i]) for i, (_, mid, dst) in enumerate(moves)]
    for copy in ins:
        copy.start()
    for before, after in zip(ins, outs):
        before.wait()
        after.start()
    for copy in outs:
        copy.wait()


def shards(fields, filter_weight, cotangent):
    rows, width, nlon = fields.shape
    if (rows, width, nlon) != (ROWS, WIDTH, NLON) or lax.axis_size("spatial") != N:
        raise ValueError("unexpected sizes")
    held = constants()
    names = ("forward", "inverse", "row_weights", "col_weights", "maps", "diag", "coef")
    flat = rows * width
    dma, vmem = pltpu.SemaphoreType.DMA, pltpu.VMEM
    shapes = (
        jax.ShapeDtypeStruct((flat, nlon), BF16),
        jax.ShapeDtypeStruct((flat, nlon), BF16),
        jax.ShapeDtypeStruct((2 * width, NLAT), F32),
    )
    results = pl.pallas_call(
        kernel,
        out_shape=shapes,
        in_specs=[pl.BlockSpec(memory_space=pl.ANY)] * 10,
        out_specs=(pl.BlockSpec(memory_space=pl.ANY),) * 3,
        scratch_shapes=[
            vmem((flat, nlon), BF16), vmem((flat, nlon), BF16), vmem((2 * width, NLAT), F32),
            vmem((2 * NLAT, nlon), BF16), vmem((2 * NLAT, nlon), BF16), vmem((16, 128), F32),
            vmem((Q, 256, 128), F32), vmem((32, 256), F32), vmem((16, 256), F32), vmem((64, 256), F32),
            vmem((N * PART, 128), F32), vmem((4, Q, N, PART, 128), BF16), vmem((4, Q, N, PART, 128), BF16),
            vmem((16 * NLAT, 128), F32), vmem((16 * NLAT, 128), F32),
            vmem((Q * GROUPS, NLAT, 256), BF16), vmem((Q * GROUPS, 256, NLAT), BF16),
            vmem((GROUPS, NLAT, 512), F32), vmem((GROUPS, NLAT, 512), F32), vmem((GROUPS, NLAT, 512), BF16),
            vmem((2, NLAT, 128), F32), vmem((256, nlon), F32),
            vmem((2, 256, NLAT), BF16), vmem((flat, nlon), BF16), vmem((flat, nlon), BF16),
            vmem((N, 16, 128), BF16), vmem((N, 16, 128), BF16), vmem((16, 128), BF16), vmem((N, 16, 128), BF16),
            vmem((2, NLAT, 128), F32), vmem((2 * width, NLAT), F32),
            dma((12,)), dma((7,)), dma((4, Q)), dma((4, Q)), dma((2,)), dma((2,)),
        ],
        compiler_params=pltpu.CompilerParams(
            collective_id=0, has_side_effects=True, vmem_limit_bytes=56 << 20
        ),
    )(
        fields.reshape(flat, nlon), cotangent.reshape(flat, nlon), filter_weight.reshape(2 * width, NLAT),
        *(jnp.asarray(held[name]) for name in names),
    )
    activated, grad_fields, grad_weight = pl.pallas_call(
        hand_over,
        out_shape=shapes,
        in_specs=[pl.BlockSpec(memory_space=pl.ANY)] * 3,
        out_specs=(pl.BlockSpec(memory_space=pl.ANY),) * 3,
        scratch_shapes=[
            vmem((flat, nlon), BF16), vmem((flat, nlon), BF16), vmem((2 * width, NLAT), F32), dma((2, 2 * Q + 1)),
        ],
    )(*results)
    return (
        activated.reshape(rows, width, nlon), grad_fields.reshape(rows, width, nlon),
        grad_weight.reshape(2, width, NLAT),
    )


def solution(mesh):
    in_specs = (P("spatial", "dp", None), P(None, "dp", None), P("spatial", "dp", None))
    out_specs = (P("spatial", "dp", None), P("spatial", "dp", None), P(None, "dp", None))
    return jax.shard_map(shards, mesh=mesh, in_specs=in_specs, out_specs=out_specs, check_vma=False)
```

```python
import functools
import math

import jax
import jax.numpy as jnp
import ml_dtypes
import numpy as np
from jax import lax
from jax.experimental import pallas as pl
from jax.experimental.pallas import tpu as pltpu
from jax.sharding import PartitionSpec as P

MESH = pl.DeviceIdType.MESH
F32, BF16 = jnp.float32, jnp.bfloat16

N = 16
ROWS = 12
WIDTH = 64
NLAT = N * ROWS
NLON = 768
Q = 3
GROUPS = 3
PART = 48
OFFSETS = sorted(
    (divmod(s, 4) for s in range(1, N)), key=lambda o: -min(o[0], 4 - o[0]) - min(o[1], 4 - o[1])
)


@functools.lru_cache(None)
def constants():
    f32, bf16 = np.float32, ml_dtypes.bfloat16
    orders = np.arange(NLAT)
    angle = 2.0 * np.pi / NLON * (orders[:, None] * np.arange(NLON)[None, :] % NLON)
    parts = np.concatenate([np.cos(angle), -np.sin(angle)], axis=0)
    factor = np.where(orders == 0, 1.0, 2.0)[:, None]
    forward = (2.0 * np.pi / NLON * parts).astype(bf16)
    inverse = (np.concatenate([factor, factor], axis=0) * parts).astype(bf16)

    theta = np.pi * (np.arange(NLAT) + 0.5) / NLAT
    cosine, sine = np.cos(theta), np.sin(theta)
    weights = np.pi / NLAT * sine
    row_weights = np.zeros((N, 16, 128), f32)
    row_weights[:, :ROWS] = weights.reshape(N, ROWS, 1)

    lane = np.arange(256)
    s, i, r = lane // 16, lane % 16 // 4, lane % 4
    rows_of = [ROWS * s + 4 * q + r for q in range(Q)]
    col_weights = np.stack([np.repeat(weights[j][:, None], 128, 1) for j in rows_of]).astype(f32)

    diagonal = np.zeros((NLAT, NLAT))
    diagonal[0] = 1.0 / math.sqrt(4.0 * math.pi)
    for m in range(1, NLAT):
        diagonal[m] = -math.sqrt((2.0 * m + 1.0) / (2.0 * m)) * sine * diagonal[m - 1]
    m, l = np.arange(NLAT)[:, None].astype(float), np.arange(NLAT)[None, :].astype(float)
    above = l > m
    scale = np.sqrt(np.where(above, 4 * l * l - 1, 0.0) / np.where(above, l * l - m * m, 1.0))
    last = l - 1
    two = last > m
    scale_last = np.sqrt(np.where(two, 4 * last * last - 1, 1.0) / np.where(two, last * last - m * m, 1.0))
    back = np.where(two, scale / scale_last, 0.0)

    cos_map = np.zeros((16, 256), f32)
    order_map = np.full((16, 256), -1.0, f32)
    diag_map = np.zeros((N, 16, 256), f32)
    coef = np.zeros((N, 64, 256), f32)
    for q in range(Q):
        for g in range(GROUPS):
            cos_map[4 * q + g] = cosine[rows_of[q]]
            order_map[4 * q + g] = 4 * g + i
            for d in range(N):
                diag_map[d, 4 * q + g] = diagonal[ROWS * d + 4 * g + i, rows_of[q]]
    for g in range(GROUPS):
        for k in range(4):
            for d in range(N):
                for kind, values in enumerate((scale, back)):
                    for copy in range(2):
                        coef[d, 32 * kind + 8 * k + 4 * copy + g, :NLAT] = values[ROWS * d + 4 * g + k]
    maps = np.concatenate([cos_map, order_map], axis=0)
    return dict(
        forward=forward, inverse=inverse, row_weights=row_weights, col_weights=col_weights,
        maps=maps, diag=diag_map, coef=coef,
    )


def kernel(
    x_hbm, cot_hbm, weight_hbm, ft_hbm, gt_hbm, roww_hbm, colw_hbm, maps_hbm, diag_hbm, coef_hbm,
    act_ref, gf_ref, gw_ref,
    xv, cotv, weightv, ftv, gtv, rowwv, colwv, mapsv, diagv, coefv,
    stage, send, recv, legendre0, legendre1, table, table_t, coeffs, dcoeffs, filtered, rotated, prev, tt, dprev,
    gsend, grecv, gout, gall, sums,
    load_sem, send_a, recv_a, send_r, recv_r,
):
    dp, me = lax.axis_index("dp"), lax.axis_index("spatial")
    mx, my = me // 4, lax.rem(me, 4)
    at = lambda dx, dy: lax.rem(mx + dx, 4) * 4 + lax.rem(my + dy, 4)
    peer_of = lambda s: lax.rem(me + s, N)

    def each_peer(action):
        def one(s, _):
            action(peer_of(s))
            return 0

        lax.fori_loop(1, N, one, 0)

    barrier = pltpu.get_barrier_semaphore()
    for dx, dy in OFFSETS:
        pl.semaphore_signal(barrier, inc=1, device_id=(dp, at(dx, dy)), device_id_type=MESH)

    quad = lambda q: pl.ds(pl.multiple_of(q * 256, 256), 256)

    def x_load(q):
        return pltpu.make_async_copy(x_hbm.at[quad(q)], xv.at[quad(q)], load_sem.at[q])

    loads = [
        pltpu.make_async_copy(src, dst, load_sem.at[3 + i])
        for i, (src, dst) in enumerate((
            (ft_hbm, ftv), (roww_hbm.at[me], rowwv), (coef_hbm.at[me], coefv),
            (diag_hbm.at[me], diagv), (maps_hbm, mapsv), (weight_hbm, weightv), (gt_hbm, gtv),
            (cot_hbm, cotv), (colw_hbm, colwv),
        ))
    ]
    loads[0].start()
    x_load(0).start()
    loads[1].start()
    x_load(1).start()
    x_load(2).start()
    for load in loads[2:5]:
        load.start()

    low = lax.broadcasted_iota(jnp.int32, (1, 128), 1) < WIDTH
    half = lambda value: pltpu.roll(value, WIDTH, 1)

    def outgoing(phase, q, peer):
        return pltpu.make_async_remote_copy(
            src_ref=send.at[phase, q, peer], dst_ref=recv.at[phase, q, me],
            send_sem=send_a.at[phase, q], recv_sem=recv_a.at[phase, q],
            device_id=(dp, peer), device_id_type=MESH,
        )

    def whole(phase, q):
        return pltpu.make_async_remote_copy(
            src_ref=send.at[phase, q, pl.ds(0, N - 1)], dst_ref=recv.at[phase, q, pl.ds(0, N - 1)],
            send_sem=send_a.at[phase, q], recv_sem=recv_a.at[phase, q],
            device_id=(dp, peer_of(1)), device_id_type=MESH,
        )

    def ship(phase, q):
        for dx, dy in OFFSETS:
            outgoing(phase, q, at(dx, dy)).start()
        recv[phase, q, me] = send[phase, q, me]

    def fourier(phase, q, rows_ref, factors, scaled):
        block = rows_ref[quad(q), :]
        out = lax.dot_general(factors[...], block, (((1,), (1,)), ((), ())), preferred_element_type=F32)
        for u in range(2):
            real, imag = out[:NLAT, 128 * u : 128 * u + 128], out[NLAT:, 128 * u : 128 * u + 128]
            pair = (jnp.where(low, real, half(imag)), jnp.where(low, half(real), imag))
            for i, value in enumerate(pair):
                r = 2 * u + i
                if scaled:
                    value = value * rowwv[pl.ds(4 * q + r, 1), :]
                stage[pl.ds(r, NLAT, stride=4), :] = value
        send[phase, q] = stage[...].astype(BF16).reshape(N, PART, 128)

    loads[0].wait()
    loads[1].wait()
    x_load(0).wait()
    fourier(0, 0, xv, ftv, True)
    pl.semaphore_wait(barrier, N - 1)
    ship(0, 0)
    for load in loads[5:]:
        load.start()

    def spectra(q, _):
        x_load(q).wait()
        fourier(0, q, xv, ftv, True)
        ship(0, q)
        return 0

    lax.fori_loop(1, Q, spectra, 0)

    for load in loads[2:5]:
        load.wait()
    order_of_lane = lax.broadcasted_iota(jnp.int32, (1, 128), 1) % 16 // 4
    first = (ROWS * me).astype(F32)

    for h in range(2):
        def degrees(g, carry, h=h):
            turned = pltpu.roll(coefv[:, 128 * h : 128 * h + 128], lax.rem(128 - 32 * g, 128), 1)
            for i in range(32):
                l = 128 * h + 32 * g + i
                pick = lambda k: jnp.broadcast_to(turned[8 * k : 8 * k + 8, i : i + 1], (8, 128))
                choose = lambda k: jnp.where(
                    order_of_lane < 2,
                    jnp.where(order_of_lane == 0, pick(k), pick(k + 1)),
                    jnp.where(order_of_lane == 2, pick(k + 2), pick(k + 3)),
                )
                scale, back = choose(0), choose(4)
                scale, back = jnp.concatenate([scale, scale], axis=0), jnp.concatenate([back, back], axis=0)
                new = []
                for u, store in ((0, legendre0), (1, legendre1)):
                    cols = slice(128 * u, 128 * u + 128)
                    last, before = carry[2 * u], carry[2 * u + 1]
                    start = jnp.where(mapsv[16:, cols] + first == l.astype(F32), diagv[:, cols], 0.0)
                    value = (scale * mapsv[:16, cols]) * last + (start - back * before)
                    store[pl.ds(l, 16, stride=NLAT), :] = value
                    new += [value, last]
                carry = tuple(new)
            return carry

        if h == 0:
            carry = (jnp.zeros((16, 128), F32),) * 4
        carry = lax.fori_loop(0, 4 if h == 0 else 2, degrees, carry)

    def finish(v, _):
        rows = pl.ds(pl.multiple_of((4 * (v // GROUPS) + lax.rem(v, GROUPS)) * NLAT, NLAT), NLAT)
        for u, store in ((0, legendre0), (1, legendre1)):
            part = store[rows, :].astype(BF16)
            table[v, :, 128 * u : 128 * u + 128] = part
        return 0

    lax.fori_loop(0, Q * GROUPS, finish, 0)

    for load in loads[5:]:
        load.wait()
    weights = weightv[...].T
    rotated[0] = jnp.where(low, weights, half(weights))
    rotated[1] = jnp.where(low, -half(weights), weights)
    coeffs[...] = jnp.zeros_like(coeffs)
    dcoeffs[...] = jnp.zeros_like(dcoeffs)
    sums[...] = jnp.zeros_like(sums)

    order_of_row = lax.broadcasted_iota(jnp.int32, (256, 128), 0) % 16 // 4
    upper = lax.broadcasted_iota(jnp.int32, (1, 8, 128), 1) < 4
    tile = lambda g: pl.ds(g * 16, 16)

    def analyse(phase, q, into):
        whole(phase, q).wait_recv()

        def one(g, _):
            block = recv[phase, q, :, tile(g), :].reshape(256, 128)
            zero = jnp.zeros_like(block)
            spread = jnp.concatenate([jnp.where(order_of_row == k, block, zero) for k in range(4)], axis=1)
            into[g] = into[g] + jnp.dot(table[GROUPS * q + g], spread, preferred_element_type=F32)
            return 0

        for g in range(GROUPS):
            one(g, 0)
        return 0

    def synthesize(phase, q, scaled):
        def one(g, _):
            out = jnp.dot(table_t[GROUPS * q + g], filtered[g], preferred_element_type=F32)
            parts = [out[:, 128 * k : 128 * k + 128].reshape(N, 2, 8, 128) for k in range(4)]
            first_half = jnp.where(upper, parts[0][:, 0], parts[1][:, 0])
            second_half = jnp.where(upper, parts[2][:, 1], parts[3][:, 1])
            out = jnp.concatenate([first_half, second_half], axis=1)
            if scaled:
                out = out * colwv[q].reshape(N, 16, 128)
            send[phase, q, :, tile(g), :] = out.astype(BF16)
            return 0

        for g in range(GROUPS):
            one(g, 0)
        ship(phase, q)
        return 0

    def turn_table(v, _):
        table_t[v] = table[v].T
        return 0

    def forward_chunk(q, _):
        analyse(0, q, coeffs)

        @pl.when(q == 1)
        def _():
            lax.fori_loop(0, Q * GROUPS, turn_table, 0)

        return 0

    lax.fori_loop(0, Q, forward_chunk, 0)

    def filter_group(g, _):
        for k in range(4):
            cols = slice(128 * k, 128 * k + 128)
            value = coeffs[g, :, cols]
            filtered[g, :, cols] = (rotated[0] * value + rotated[1] * half(value)).astype(BF16)
        return 0

    for g in range(GROUPS):
        filter_group(g, 0)
    lax.fori_loop(0, Q, lambda q, _: synthesize(1, q, False), 0)

    def gather(phase, q):
        whole(phase, q).wait_recv()
        stage[...] = recv[phase, q].reshape(N * PART, 128).astype(F32)
        for r in range(4):
            turned = stage[pl.ds(r, NLAT, stride=4), :].astype(BF16).T
            tt[0, WIDTH * r : WIDTH * r + WIDTH, :] = turned[:WIDTH]
            tt[1, WIDTH * r : WIDTH * r + WIDTH, :] = turned[WIDTH:]

    def grid_rows(factors):
        return jnp.dot(tt[0], factors[:NLAT, :], preferred_element_type=F32) + jnp.dot(
            tt[1], factors[NLAT:, :], preferred_element_type=F32
        )

    def activation(q, _):
        gather(1, q)
        prev[...] = grid_rows(gtv)

        def strip(i, _):
            here = pl.ds(pl.multiple_of(i * 16, 16), 16)
            there = pl.ds(pl.multiple_of(q * 256 + i * 16, 16), 16)
            pre = prev[here, :]
            cdf = 0.5 + 0.5 * lax.erf(pre * (1.0 / math.sqrt(2.0)))
            density = jnp.exp(-0.5 * pre * pre) * (1.0 / math.sqrt(2.0 * math.pi))
            act_ref[there, :] = (pre * cdf).astype(BF16)
            dprev[there, :] = (cotv[there, :].astype(F32) * (cdf + pre * density)).astype(BF16)
            return 0

        lax.fori_loop(0, 16, strip, 0)
        fourier(2, q, dprev, gtv, False)
        ship(2, q)
        return 0

    lax.fori_loop(0, Q, activation, 0)

    lax.fori_loop(0, Q, lambda q, _: analyse(2, q, dcoeffs), 0)

    def sum_group(g, _):
        for k in range(4):
            cols = slice(128 * k, 128 * k + 128)
            value, coeff = dcoeffs[g, :, cols], coeffs[g, :, cols]
            sums[0] = sums[0] + value * coeff
            sums[1] = sums[1] + value * half(coeff)
        return 0

    lax.fori_loop(0, GROUPS, sum_group, 0)
    same, cross = sums[0], sums[1]
    partial = jnp.where(low, same + half(same), cross - half(cross)).astype(BF16)
    gsend[:ROWS] = partial.reshape(ROWS, 16, 128)
    gsend[ROWS:] = jnp.zeros((N - ROWS, 16, 128), BF16)

    def small_copy(turn, peer):
        return pltpu.make_async_remote_copy(
            src_ref=gout if turn else gsend.at[peer], dst_ref=(gall if turn else grecv).at[me],
            send_sem=send_r.at[turn], recv_sem=recv_r.at[turn],
            device_id=(dp, peer), device_id_type=MESH,
        )

    def small_whole(turn):
        ref = (gall if turn else grecv).at[pl.ds(0, N - 1)]
        return pltpu.make_async_remote_copy(
            src_ref=gsend.at[pl.ds(0, N - 1)], dst_ref=ref, send_sem=send_r.at[turn], recv_sem=recv_r.at[turn],
            device_id=(dp, peer_of(1)), device_id_type=MESH,
        )

    each_peer(lambda peer: small_copy(0, peer).start())
    grecv[me] = gsend[me]
    def adjoint_group(g, _):
        for k in range(4):
            cols = slice(128 * k, 128 * k + 128)
            value = dcoeffs[g, :, cols]
            filtered[g, :, cols] = (rotated[0] * value - rotated[1] * half(value)).astype(BF16)
        return 0

    for g in range(GROUPS):
        adjoint_group(g, 0)
    synthesize(3, 0, True)

    synthesize(3, 1, True)
    synthesize(3, 2, True)
    small_whole(0).wait_recv()
    total = (jnp.sum(grecv[...].astype(F32), axis=0) * (1.0 / NLAT)).astype(BF16)
    gout[...] = total
    gall[me] = total
    each_peer(lambda peer: small_copy(1, peer).start())

    def gradient(q, _):
        gather(3, q)
        gf_ref[quad(q), :] = grid_rows(ftv).astype(BF16)
        return 0

    lax.fori_loop(0, Q, gradient, 0)

    small_whole(1).wait_recv()
    gw_ref[...] = gall[:ROWS].reshape(NLAT, 128).astype(F32).T

    for phase in range(4):
        for q in range(Q):
            whole(phase, q).wait_send()
    for turn in range(2):
        small_whole(turn).wait_send()


def hand_over(act, gf, gw, act_out, gf_out, gw_out, sems):
    moves = ((act, act_out), (gf, gf_out), (gw, gw_out))
    copies = [pltpu.make_async_copy(src, dst, sems.at[i]) for i, (src, dst) in enumerate(moves)]
    for copy in copies:
        copy.start()
    for copy in copies:
        copy.wait()


def shards(fields, filter_weight, cotangent):
    rows, width, nlon = fields.shape
    if (rows, width, nlon) != (ROWS, WIDTH, NLON) or lax.axis_size("spatial") != N:
        raise ValueError("unexpected sizes")
    held = constants()
    names = ("forward", "inverse", "row_weights", "col_weights", "maps", "diag", "coef")
    flat = rows * width
    dma, vmem = pltpu.SemaphoreType.DMA, pltpu.VMEM
    shapes = (
        jax.ShapeDtypeStruct((flat, nlon), BF16),
        jax.ShapeDtypeStruct((flat, nlon), BF16),
        jax.ShapeDtypeStruct((2 * width, NLAT), F32),
    )
    results = pl.pallas_call(
        kernel,
        out_shape=tuple(vmem(shape.shape, shape.dtype) for shape in shapes),
        in_specs=[pl.BlockSpec(memory_space=pl.ANY)] * 10,
        out_specs=(pl.BlockSpec(memory_space=pltpu.VMEM),) * 3,
        scratch_shapes=[
            vmem((flat, nlon), BF16), vmem((flat, nlon), BF16), vmem((2 * width, NLAT), F32),
            vmem((2 * NLAT, nlon), BF16), vmem((2 * NLAT, nlon), BF16), vmem((16, 128), F32),
            vmem((Q, 256, 128), F32), vmem((32, 256), F32), vmem((16, 256), F32), vmem((64, 256), F32),
            vmem((N * PART, 128), F32), vmem((4, Q, N, PART, 128), BF16), vmem((4, Q, N, PART, 128), BF16),
            vmem((16 * NLAT, 128), F32), vmem((16 * NLAT, 128), F32),
            vmem((Q * GROUPS, NLAT, 256), BF16), vmem((Q * GROUPS, 256, NLAT), BF16),
            vmem((GROUPS, NLAT, 512), F32), vmem((GROUPS, NLAT, 512), F32), vmem((GROUPS, NLAT, 512), BF16),
            vmem((2, NLAT, 128), F32), vmem((256, nlon), F32),
            vmem((2, 256, NLAT), BF16), vmem((flat, nlon), BF16),
            vmem((N, 16, 128), BF16), vmem((N, 16, 128), BF16), vmem((16, 128), BF16), vmem((N, 16, 128), BF16),
            vmem((2, NLAT, 128), F32),
            dma((12,)), dma((4, Q)), dma((4, Q)), dma((2,)), dma((2,)),
        ],
        compiler_params=pltpu.CompilerParams(
            collective_id=0, has_side_effects=True, vmem_limit_bytes=56 << 20
        ),
    )(
        fields.reshape(flat, nlon), cotangent.reshape(flat, nlon), filter_weight.reshape(2 * width, NLAT),
        *(jnp.asarray(held[name]) for name in names),
    )
    activated, grad_fields, grad_weight = pl.pallas_call(
        hand_over,
        out_shape=shapes,
        in_specs=[pl.BlockSpec(memory_space=pltpu.VMEM)] * 3,
        out_specs=(pl.BlockSpec(memory_space=pl.ANY),) * 3,
        scratch_shapes=[dma((3,))],
    )(*(pltpu.with_memory_space_constraint(result, pltpu.VMEM) for result in results))
    return (
        activated.reshape(rows, width, nlon), grad_fields.reshape(rows, width, nlon),
        grad_weight.reshape(2, width, NLAT),
    )


def solution(mesh):
    in_specs = (P("spatial", "dp", None), P(None, "dp", None), P("spatial", "dp", None))
    out_specs = (P("spatial", "dp", None), P("spatial", "dp", None), P(None, "dp", None))
    return jax.shard_map(shards, mesh=mesh, in_specs=in_specs, out_specs=out_specs, check_vma=False)
```

```python
import functools
import math

import jax
import jax.numpy as jnp
import ml_dtypes
import numpy as np
from jax import lax
from jax.experimental import pallas as pl
from jax.experimental.pallas import tpu as pltpu
from jax.sharding import PartitionSpec as P

MESH = pl.DeviceIdType.MESH
F32, BF16 = jnp.float32, jnp.bfloat16

N = 16
ROWS = 12
WIDTH = 64
NLAT = N * ROWS
NLON = 768
Q = 3
GROUPS = 3
PART = 48
OFFSETS = sorted(
    (divmod(s, 4) for s in range(1, N)), key=lambda o: -min(o[0], 4 - o[0]) - min(o[1], 4 - o[1])
)


@functools.lru_cache(None)
def constants():
    f32, bf16 = np.float32, ml_dtypes.bfloat16
    orders = np.arange(NLAT)
    angle = 2.0 * np.pi / NLON * (orders[:, None] * np.arange(NLON)[None, :] % NLON)
    parts = np.concatenate([np.cos(angle), -np.sin(angle)], axis=0)
    factor = np.where(orders == 0, 1.0, 2.0)[:, None]
    forward = (2.0 * np.pi / NLON * parts).astype(bf16)
    inverse = (np.concatenate([factor, factor], axis=0) * parts).astype(bf16)

    theta = np.pi * (np.arange(NLAT) + 0.5) / NLAT
    cosine, sine = np.cos(theta), np.sin(theta)
    weights = np.pi / NLAT * sine
    row_weights = np.zeros((N, 16, 128), f32)
    row_weights[:, :ROWS] = weights.reshape(N, ROWS, 1)

    lane = np.arange(256)
    s, i, r = lane // 16, lane % 16 // 4, lane % 4
    rows_of = [ROWS * s + 4 * q + r for q in range(Q)]
    col_weights = np.stack([np.repeat(weights[j][:, None], 128, 1) for j in rows_of]).astype(f32)

    diagonal = np.zeros((NLAT, NLAT))
    diagonal[0] = 1.0 / math.sqrt(4.0 * math.pi)
    for m in range(1, NLAT):
        diagonal[m] = -math.sqrt((2.0 * m + 1.0) / (2.0 * m)) * sine * diagonal[m - 1]
    m, l = np.arange(NLAT)[:, None].astype(float), np.arange(NLAT)[None, :].astype(float)
    above = l > m
    scale = np.sqrt(np.where(above, 4 * l * l - 1, 0.0) / np.where(above, l * l - m * m, 1.0))
    last = l - 1
    two = last > m
    scale_last = np.sqrt(np.where(two, 4 * last * last - 1, 1.0) / np.where(two, last * last - m * m, 1.0))
    back = np.where(two, scale / scale_last, 0.0)

    cos_map = np.zeros((16, 256), f32)
    order_map = np.full((16, 256), -1.0, f32)
    diag_map = np.zeros((N, 16, 256), f32)
    coef = np.zeros((N, 64, 256), f32)
    for q in range(Q):
        for g in range(GROUPS):
            cos_map[4 * q + g] = cosine[rows_of[q]]
            order_map[4 * q + g] = 4 * g + i
            for d in range(N):
                diag_map[d, 4 * q + g] = diagonal[ROWS * d + 4 * g + i, rows_of[q]]
    for g in range(GROUPS):
        for k in range(4):
            for d in range(N):
                for kind, values in enumerate((scale, back)):
                    for copy in range(2):
                        coef[d, 32 * kind + 8 * k + 4 * copy + g, :NLAT] = values[ROWS * d + 4 * g + k]
    maps = np.concatenate([cos_map, order_map], axis=0)
    return dict(
        forward=forward, inverse=inverse, row_weights=row_weights, col_weights=col_weights,
        maps=maps, diag=diag_map, coef=coef,
    )


def kernel(
    x_hbm, cot_hbm, weight_hbm, ft_hbm, gt_hbm, roww_hbm, colw_hbm, maps_hbm, diag_hbm, coef_hbm,
    act_ref, gf_ref, gw_ref,
    xv, cotv, weightv, ftv, gtv, rowwv, colwv, mapsv, diagv, coefv,
    stage, send, recv, legendre0, legendre1, table, table_t, coeffs, dcoeffs, filtered, rotated, prev, tt, dprev,
    gsend, grecv, gout, gall,
    load_sem, send_a, recv_a, send_r, recv_r,
):
    dp, me = lax.axis_index("dp"), lax.axis_index("spatial")
    mx, my = me // 4, lax.rem(me, 4)
    at = lambda dx, dy: lax.rem(mx + dx, 4) * 4 + lax.rem(my + dy, 4)
    peers = [at(dx, dy) for dx, dy in OFFSETS]

    barrier = pltpu.get_barrier_semaphore()
    for peer in peers:
        pl.semaphore_signal(barrier, inc=1, device_id=(dp, peer), device_id_type=MESH)

    quad = lambda q: pl.ds(pl.multiple_of(q * 256, 256), 256)

    def x_load(q):
        return pltpu.make_async_copy(x_hbm.at[quad(q)], xv.at[quad(q)], load_sem.at[q])

    loads = [
        pltpu.make_async_copy(src, dst, load_sem.at[3 + i])
        for i, (src, dst) in enumerate((
            (ft_hbm, ftv), (roww_hbm.at[me], rowwv), (coef_hbm.at[me], coefv),
            (diag_hbm.at[me], diagv), (maps_hbm, mapsv), (weight_hbm, weightv), (gt_hbm, gtv),
            (cot_hbm, cotv), (colw_hbm, colwv),
        ))
    ]
    loads[0].start()
    x_load(0).start()
    loads[1].start()
    x_load(1).start()
    x_load(2).start()
    for load in loads[2:5]:
        load.start()

    low = lax.broadcasted_iota(jnp.int32, (1, 128), 1) < WIDTH
    half = lambda value: pltpu.roll(value, WIDTH, 1)

    def outgoing(phase, q, peer):
        return pltpu.make_async_remote_copy(
            src_ref=send.at[phase, q, peer], dst_ref=recv.at[phase, q, me],
            send_sem=send_a.at[phase, q], recv_sem=recv_a.at[phase, q],
            device_id=(dp, peer), device_id_type=MESH,
        )

    def whole(phase, q):
        return pltpu.make_async_remote_copy(
            src_ref=send.at[phase, q, pl.ds(0, N - 1)], dst_ref=recv.at[phase, q, pl.ds(0, N - 1)],
            send_sem=send_a.at[phase, q], recv_sem=recv_a.at[phase, q],
            device_id=(dp, peers[0]), device_id_type=MESH,
        )

    def ship(phase, q):
        for peer in peers:
            outgoing(phase, q, peer).start()
        recv[phase, q, me] = send[phase, q, me]

    def fourier(phase, q, rows_ref, factors, scaled):
        block = rows_ref[quad(q), :]
        out = lax.dot_general(factors[...], block, (((1,), (1,)), ((), ())), preferred_element_type=F32)
        for u in range(2):
            real, imag = out[:NLAT, 128 * u : 128 * u + 128], out[NLAT:, 128 * u : 128 * u + 128]
            pair = (jnp.where(low, real, half(imag)), jnp.where(low, half(real), imag))
            for i, value in enumerate(pair):
                r = 2 * u + i
                if scaled:
                    value = value * rowwv[pl.ds(4 * q + r, 1), :]
                stage[pl.ds(r, NLAT, stride=4), :] = value
        send[phase, q] = stage[...].astype(BF16).reshape(N, PART, 128)

    loads[0].wait()
    loads[1].wait()
    x_load(0).wait()
    fourier(0, 0, xv, ftv, True)
    pl.semaphore_wait(barrier, N - 1)
    ship(0, 0)
    for load in loads[5:]:
        load.start()

    def spectra(q, _):
        x_load(q).wait()
        fourier(0, q, xv, ftv, True)
        ship(0, q)
        return 0

    lax.fori_loop(1, Q, spectra, 0)

    for load in loads[2:5]:
        load.wait()
    order_of_lane = lax.broadcasted_iota(jnp.int32, (1, 128), 1) % 16 // 4
    first = (ROWS * me).astype(F32)

    for h in range(2):
        def degrees(g, carry, h=h):
            turned = pltpu.roll(coefv[:, 128 * h : 128 * h + 128], lax.rem(128 - 32 * g, 128), 1)
            for i in range(32):
                l = 128 * h + 32 * g + i
                pick = lambda k: jnp.broadcast_to(turned[8 * k : 8 * k + 8, i : i + 1], (8, 128))
                choose = lambda k: jnp.where(
                    order_of_lane < 2,
                    jnp.where(order_of_lane == 0, pick(k), pick(k + 1)),
                    jnp.where(order_of_lane == 2, pick(k + 2), pick(k + 3)),
                )
                scale, back = choose(0), choose(4)
                scale, back = jnp.concatenate([scale, scale], axis=0), jnp.concatenate([back, back], axis=0)
                new = []
                for u, store in ((0, legendre0), (1, legendre1)):
                    cols = slice(128 * u, 128 * u + 128)
                    last, before = carry[2 * u], carry[2 * u + 1]
                    start = jnp.where(mapsv[16:, cols] + first == l.astype(F32), diagv[:, cols], 0.0)
                    value = (scale * mapsv[:16, cols]) * last + (start - back * before)
                    store[pl.ds(l, 16, stride=NLAT), :] = value
                    new += [value, last]
                carry = tuple(new)
            return carry

        if h == 0:
            carry = (jnp.zeros((16, 128), F32),) * 4
        carry = lax.fori_loop(0, 4 if h == 0 else 2, degrees, carry)

    def finish(v, _):
        rows = pl.ds(pl.multiple_of((4 * (v // GROUPS) + lax.rem(v, GROUPS)) * NLAT, NLAT), NLAT)
        for u, store in ((0, legendre0), (1, legendre1)):
            part = store[rows, :].astype(BF16)
            table[v, :, 128 * u : 128 * u + 128] = part
        return 0

    lax.fori_loop(0, Q * GROUPS, finish, 0)

    for load in loads[5:]:
        load.wait()
    weights = weightv[...].T
    rotated[0] = jnp.where(low, weights, half(weights))
    rotated[1] = jnp.where(low, -half(weights), weights)
    coeffs[...] = jnp.zeros_like(coeffs)
    dcoeffs[...] = jnp.zeros_like(dcoeffs)

    order_of_row = lax.broadcasted_iota(jnp.int32, (256, 128), 0) % 16 // 4
    upper = lax.broadcasted_iota(jnp.int32, (1, 8, 128), 1) < 4
    tile = lambda g: pl.ds(g * 16, 16)

    def analyse(phase, q, into):
        whole(phase, q).wait_recv()

        def one(g, _):
            block = recv[phase, q, :, tile(g), :].reshape(256, 128)
            zero = jnp.zeros_like(block)
            spread = jnp.concatenate([jnp.where(order_of_row == k, block, zero) for k in range(4)], axis=1)
            into[g] = into[g] + jnp.dot(table[GROUPS * q + g], spread, preferred_element_type=F32)
            return 0

        for g in range(GROUPS):
            one(g, 0)
        return 0

    def synthesize(phase, q, scaled):
        def one(g, _):
            out = jnp.dot(table_t[GROUPS * q + g], filtered[g], preferred_element_type=F32)
            parts = [out[:, 128 * k : 128 * k + 128].reshape(N, 2, 8, 128) for k in range(4)]
            first_half = jnp.where(upper, parts[0][:, 0], parts[1][:, 0])
            second_half = jnp.where(upper, parts[2][:, 1], parts[3][:, 1])
            out = jnp.concatenate([first_half, second_half], axis=1)
            if scaled:
                out = out * colwv[q].reshape(N, 16, 128)
            send[phase, q, :, tile(g), :] = out.astype(BF16)
            return 0

        for g in range(GROUPS):
            one(g, 0)
        ship(phase, q)
        return 0

    def turn_table(v, _):
        table_t[v] = table[v].T
        return 0

    def forward_chunk(q, _):
        analyse(0, q, coeffs)

        @pl.when(q == 1)
        def _():
            lax.fori_loop(0, Q * GROUPS, turn_table, 0)

        return 0

    lax.fori_loop(0, Q, forward_chunk, 0)

    def filter_group(g, _):
        for k in range(4):
            cols = slice(128 * k, 128 * k + 128)
            value = coeffs[g, :, cols]
            filtered[g, :, cols] = (rotated[0] * value + rotated[1] * half(value)).astype(BF16)
        return 0

    for g in range(GROUPS):
        filter_group(g, 0)
    lax.fori_loop(0, Q, lambda q, _: synthesize(1, q, False), 0)

    def gather(phase, q):
        whole(phase, q).wait_recv()
        stage[...] = recv[phase, q].reshape(N * PART, 128).astype(F32)
        for r in range(4):
            turned = stage[pl.ds(r, NLAT, stride=4), :].astype(BF16).T
            tt[0, WIDTH * r : WIDTH * r + WIDTH, :] = turned[:WIDTH]
            tt[1, WIDTH * r : WIDTH * r + WIDTH, :] = turned[WIDTH:]

    def grid_rows(factors):
        return jnp.dot(tt[0], factors[:NLAT, :], preferred_element_type=F32) + jnp.dot(
            tt[1], factors[NLAT:, :], preferred_element_type=F32
        )

    def activation(q, _):
        gather(1, q)
        prev[...] = grid_rows(gtv)

        def strip(i, _):
            here = pl.ds(pl.multiple_of(i * 16, 16), 16)
            there = pl.ds(pl.multiple_of(q * 256 + i * 16, 16), 16)
            pre = prev[here, :]
            cdf = 0.5 + 0.5 * lax.erf(pre * (1.0 / math.sqrt(2.0)))
            density = jnp.exp(-0.5 * pre * pre) * (1.0 / math.sqrt(2.0 * math.pi))
            act_ref[there, :] = (pre * cdf).astype(BF16)
            dprev[there, :] = (cotv[there, :].astype(F32) * (cdf + pre * density)).astype(BF16)
            return 0

        lax.fori_loop(0, 16, strip, 0)
        fourier(2, q, dprev, gtv, False)
        ship(2, q)
        return 0

    lax.fori_loop(0, Q, activation, 0)

    lax.fori_loop(0, Q, lambda q, _: analyse(2, q, dcoeffs), 0)

    places = [(g, slice(None), slice(128 * k, 128 * k + 128)) for g in range(GROUPS) for k in range(4)]
    same = sum(dcoeffs[place] * coeffs[place] for place in places)
    cross = sum(dcoeffs[place] * half(coeffs[place]) for place in places)
    partial = jnp.where(low, same + half(same), cross - half(cross)).astype(BF16)
    gsend[:ROWS] = partial.reshape(ROWS, 16, 128)
    gsend[ROWS:] = jnp.zeros((N - ROWS, 16, 128), BF16)

    def small_copy(turn, peer):
        return pltpu.make_async_remote_copy(
            src_ref=gout if turn else gsend.at[peer], dst_ref=(gall if turn else grecv).at[me],
            send_sem=send_r.at[turn], recv_sem=recv_r.at[turn],
            device_id=(dp, peer), device_id_type=MESH,
        )

    def small_whole(turn):
        ref = (gall if turn else grecv).at[pl.ds(0, N - 1)]
        return pltpu.make_async_remote_copy(
            src_ref=gsend.at[pl.ds(0, N - 1)], dst_ref=ref, send_sem=send_r.at[turn], recv_sem=recv_r.at[turn],
            device_id=(dp, peers[0]), device_id_type=MESH,
        )

    for peer in peers:
        small_copy(0, peer).start()
    grecv[me] = gsend[me]
    def adjoint_group(g, _):
        for k in range(4):
            cols = slice(128 * k, 128 * k + 128)
            value = dcoeffs[g, :, cols]
            filtered[g, :, cols] = (rotated[0] * value - rotated[1] * half(value)).astype(BF16)
        return 0

    for g in range(GROUPS):
        adjoint_group(g, 0)
    synthesize(3, 0, True)

    synthesize(3, 1, True)
    synthesize(3, 2, True)
    small_whole(0).wait_recv()
    total = (jnp.sum(grecv[...].astype(F32), axis=0) * (1.0 / NLAT)).astype(BF16)
    gout[...] = total
    gall[me] = total
    for peer in peers:
        small_copy(1, peer).start()

    def gradient(q, _):
        gather(3, q)
        gf_ref[quad(q), :] = grid_rows(ftv).astype(BF16)
        return 0

    lax.fori_loop(0, Q, gradient, 0)

    small_whole(1).wait_recv()
    gw_ref[...] = gall[:ROWS].reshape(NLAT, 128).astype(F32).T

    for phase in range(4):
        for q in range(Q):
            whole(phase, q).wait_send()
    for turn in range(2):
        small_whole(turn).wait_send()


def hand_over(act, gf, gw, act_out, gf_out, gw_out, sems):
    moves = ((act, act_out), (gf, gf_out), (gw, gw_out))
    copies = [pltpu.make_async_copy(src, dst, sems.at[i]) for i, (src, dst) in enumerate(moves)]
    for copy in copies:
        copy.start()
    for copy in copies:
        copy.wait()


def shards(fields, filter_weight, cotangent):
    rows, width, nlon = fields.shape
    if (rows, width, nlon) != (ROWS, WIDTH, NLON) or lax.axis_size("spatial") != N:
        raise ValueError("unexpected sizes")
    held = constants()
    names = ("forward", "inverse", "row_weights", "col_weights", "maps", "diag", "coef")
    flat = rows * width
    dma, vmem = pltpu.SemaphoreType.DMA, pltpu.VMEM
    shapes = (
        jax.ShapeDtypeStruct((flat, nlon), BF16),
        jax.ShapeDtypeStruct((flat, nlon), BF16),
        jax.ShapeDtypeStruct((2 * width, NLAT), F32),
    )
    results = pl.pallas_call(
        kernel,
        out_shape=tuple(vmem(shape.shape, shape.dtype) for shape in shapes),
        in_specs=[pl.BlockSpec(memory_space=pl.ANY)] * 10,
        out_specs=(pl.BlockSpec(memory_space=pltpu.VMEM),) * 3,
        scratch_shapes=[
            vmem((flat, nlon), BF16), vmem((flat, nlon), BF16), vmem((2 * width, NLAT), F32),
            vmem((2 * NLAT, nlon), BF16), vmem((2 * NLAT, nlon), BF16), vmem((16, 128), F32),
            vmem((Q, 256, 128), F32), vmem((32, 256), F32), vmem((16, 256), F32), vmem((64, 256), F32),
            vmem((N * PART, 128), F32), vmem((4, Q, N, PART, 128), BF16), vmem((4, Q, N, PART, 128), BF16),
            vmem((16 * NLAT, 128), F32), vmem((16 * NLAT, 128), F32),
            vmem((Q * GROUPS, NLAT, 256), BF16), vmem((Q * GROUPS, 256, NLAT), BF16),
            vmem((GROUPS, NLAT, 512), F32), vmem((GROUPS, NLAT, 512), F32), vmem((GROUPS, NLAT, 512), BF16),
            vmem((2, NLAT, 128), F32), vmem((256, nlon), F32),
            vmem((2, 256, NLAT), BF16), vmem((flat, nlon), BF16),
            vmem((N, 16, 128), BF16), vmem((N, 16, 128), BF16), vmem((16, 128), BF16), vmem((N, 16, 128), BF16),
            dma((12,)), dma((4, Q)), dma((4, Q)), dma((2,)), dma((2,)),
        ],
        compiler_params=pltpu.CompilerParams(
            collective_id=0, has_side_effects=True, vmem_limit_bytes=56 << 20
        ),
    )(
        fields.reshape(flat, nlon), cotangent.reshape(flat, nlon), filter_weight.reshape(2 * width, NLAT),
        *(jnp.asarray(held[name]) for name in names),
    )
    activated, grad_fields, grad_weight = pl.pallas_call(
        hand_over,
        out_shape=shapes,
        in_specs=[pl.BlockSpec(memory_space=pltpu.VMEM)] * 3,
        out_specs=(pl.BlockSpec(memory_space=pl.ANY),) * 3,
        scratch_shapes=[dma((3,))],
    )(*(pltpu.with_memory_space_constraint(result, pltpu.VMEM) for result in results))
    return (
        activated.reshape(rows, width, nlon), grad_fields.reshape(rows, width, nlon),
        grad_weight.reshape(2, width, NLAT),
    )


def solution(mesh):
    in_specs = (P("spatial", "dp", None), P(None, "dp", None), P("spatial", "dp", None))
    out_specs = (P("spatial", "dp", None), P("spatial", "dp", None), P(None, "dp", None))
    return jax.shard_map(shards, mesh=mesh, in_specs=in_specs, out_specs=out_specs, check_vma=False)
```

```python
import functools
import math

import jax
import jax.numpy as jnp
import ml_dtypes
import numpy as np
from jax import lax
from jax.experimental import pallas as pl
from jax.experimental.pallas import tpu as pltpu
from jax.sharding import PartitionSpec as P

MESH = pl.DeviceIdType.MESH
F32, BF16 = jnp.float32, jnp.bfloat16

N = 16
ROWS = 12
WIDTH = 64
NLAT = N * ROWS
NLON = 768
Q = 3
GROUPS = 3
PART = 48
OFFSETS = sorted(
    (divmod(s, 4) for s in range(1, N)), key=lambda o: -min(o[0], 4 - o[0]) - min(o[1], 4 - o[1])
)


@functools.lru_cache(None)
def constants():
    f32, bf16 = np.float32, ml_dtypes.bfloat16
    orders = np.arange(NLAT)
    angle = 2.0 * np.pi / NLON * (orders[:, None] * np.arange(NLON)[None, :] % NLON)
    parts = np.concatenate([np.cos(angle), -np.sin(angle)], axis=0)
    factor = np.where(orders == 0, 1.0, 2.0)[:, None]
    forward = (2.0 * np.pi / NLON * parts).astype(bf16)
    inverse = (np.concatenate([factor, factor], axis=0) * parts).astype(bf16)

    theta = np.pi * (np.arange(NLAT) + 0.5) / NLAT
    cosine, sine = np.cos(theta), np.sin(theta)
    weights = np.pi / NLAT * sine
    row_weights = np.zeros((N, 16, 128), f32)
    row_weights[:, :ROWS] = weights.reshape(N, ROWS, 1)

    lane = np.arange(256)
    s, i, r = lane // 16, lane % 16 // 4, lane % 4
    rows_of = [ROWS * s + 4 * q + r for q in range(Q)]
    col_weights = np.stack([np.repeat(weights[j][:, None], 128, 1) for j in rows_of]).astype(f32)

    diagonal = np.zeros((NLAT, NLAT))
    diagonal[0] = 1.0 / math.sqrt(4.0 * math.pi)
    for m in range(1, NLAT):
        diagonal[m] = -math.sqrt((2.0 * m + 1.0) / (2.0 * m)) * sine * diagonal[m - 1]
    m, l = np.arange(NLAT)[:, None].astype(float), np.arange(NLAT)[None, :].astype(float)
    above = l > m
    scale = np.sqrt(np.where(above, 4 * l * l - 1, 0.0) / np.where(above, l * l - m * m, 1.0))
    last = l - 1
    two = last > m
    scale_last = np.sqrt(np.where(two, 4 * last * last - 1, 1.0) / np.where(two, last * last - m * m, 1.0))
    back = np.where(two, scale / scale_last, 0.0)

    cos_map = np.zeros((16, 256), f32)
    order_map = np.full((16, 256), -1.0, f32)
    diag_map = np.zeros((N, 16, 256), f32)
    coef = np.zeros((N, 64, 256), f32)
    for q in range(Q):
        for g in range(GROUPS):
            cos_map[4 * q + g] = cosine[rows_of[q]]
            order_map[4 * q + g] = 4 * g + i
            for d in range(N):
                diag_map[d, 4 * q + g] = diagonal[ROWS * d + 4 * g + i, rows_of[q]]
    for g in range(GROUPS):
        for k in range(4):
            for d in range(N):
                for kind, values in enumerate((scale, back)):
                    for copy in range(2):
                        coef[d, 32 * kind + 8 * k + 4 * copy + g, :NLAT] = values[ROWS * d + 4 * g + k]
    maps = np.concatenate([cos_map, order_map], axis=0)
    return dict(
        forward=forward, inverse=inverse, row_weights=row_weights, col_weights=col_weights,
        maps=maps, diag=diag_map, coef=coef,
    )


def kernel(
    x_hbm, cot_hbm, weight_hbm, ft_hbm, gt_hbm, roww_hbm, colw_hbm, maps_hbm, diag_hbm, coef_hbm,
    act_ref, gf_ref, gw_ref,
    xv, cotv, weightv, ftv, gtv, rowwv, colwv, mapsv, diagv, coefv,
    stage, send, recv, legendre0, legendre1, table, table_t, coeffs, turned, dcoeffs, filtered, rotated, prev, tt, dprev,
    gsend, grecv, gout, gall,
    load_sem, send_a, recv_a, send_r, recv_r,
):
    dp, me = lax.axis_index("dp"), lax.axis_index("spatial")
    mx, my = me // 4, lax.rem(me, 4)
    at = lambda dx, dy: lax.rem(mx + dx, 4) * 4 + lax.rem(my + dy, 4)
    peers = [at(dx, dy) for dx, dy in OFFSETS]

    barrier = pltpu.get_barrier_semaphore()
    for peer in peers:
        pl.semaphore_signal(barrier, inc=1, device_id=(dp, peer), device_id_type=MESH)

    quad = lambda q: pl.ds(pl.multiple_of(q * 256, 256), 256)

    def x_load(q):
        return pltpu.make_async_copy(x_hbm.at[quad(q)], xv.at[quad(q)], load_sem.at[q])

    loads = [
        pltpu.make_async_copy(src, dst, load_sem.at[3 + i])
        for i, (src, dst) in enumerate((
            (ft_hbm, ftv), (roww_hbm.at[me], rowwv), (coef_hbm.at[me], coefv),
            (diag_hbm.at[me], diagv), (maps_hbm, mapsv), (weight_hbm, weightv), (gt_hbm, gtv),
            (cot_hbm, cotv), (colw_hbm, colwv),
        ))
    ]
    loads[0].start()
    x_load(0).start()
    loads[1].start()
    x_load(1).start()
    x_load(2).start()
    for load in loads[2:5]:
        load.start()

    low = lax.broadcasted_iota(jnp.int32, (1, 128), 1) < WIDTH
    half = lambda value: pltpu.roll(value, WIDTH, 1)

    def outgoing(phase, q, peer):
        return pltpu.make_async_remote_copy(
            src_ref=send.at[phase, q, peer], dst_ref=recv.at[phase, q, me],
            send_sem=send_a.at[phase, q], recv_sem=recv_a.at[phase, q],
            device_id=(dp, peer), device_id_type=MESH,
        )

    def whole(phase, q):
        return pltpu.make_async_remote_copy(
            src_ref=send.at[phase, q, pl.ds(0, N - 1)], dst_ref=recv.at[phase, q, pl.ds(0, N - 1)],
            send_sem=send_a.at[phase, q], recv_sem=recv_a.at[phase, q],
            device_id=(dp, peers[0]), device_id_type=MESH,
        )

    def ship(phase, q):
        for peer in peers:
            outgoing(phase, q, peer).start()
        recv[phase, q, me] = send[phase, q, me]

    def fourier(phase, q, rows_ref, factors, scaled):
        block = rows_ref[quad(q), :]
        out = lax.dot_general(factors[...], block, (((1,), (1,)), ((), ())), preferred_element_type=F32)
        for u in range(2):
            real, imag = out[:NLAT, 128 * u : 128 * u + 128], out[NLAT:, 128 * u : 128 * u + 128]
            pair = (jnp.where(low, real, half(imag)), jnp.where(low, half(real), imag))
            for i, value in enumerate(pair):
                r = 2 * u + i
                if scaled:
                    value = value * rowwv[pl.ds(4 * q + r, 1), :]
                stage[pl.ds(r, NLAT, stride=4), :] = value
        send[phase, q] = stage[...].astype(BF16).reshape(N, PART, 128)

    loads[0].wait()
    loads[1].wait()
    x_load(0).wait()
    fourier(0, 0, xv, ftv, True)
    pl.semaphore_wait(barrier, N - 1)
    ship(0, 0)
    for load in loads[5:]:
        load.start()

    def spectra(q, _):
        x_load(q).wait()
        fourier(0, q, xv, ftv, True)
        ship(0, q)
        return 0

    lax.fori_loop(1, Q, spectra, 0)

    for load in loads[2:5]:
        load.wait()
    order_of_lane = lax.broadcasted_iota(jnp.int32, (1, 128), 1) % 16 // 4
    first = (ROWS * me).astype(F32)

    for h in range(2):
        def degrees(g, carry, h=h):
            turned = pltpu.roll(coefv[:, 128 * h : 128 * h + 128], lax.rem(128 - 32 * g, 128), 1)
            for i in range(32):
                l = 128 * h + 32 * g + i
                pick = lambda k: jnp.broadcast_to(turned[8 * k : 8 * k + 8, i : i + 1], (8, 128))
                choose = lambda k: jnp.where(
                    order_of_lane < 2,
                    jnp.where(order_of_lane == 0, pick(k), pick(k + 1)),
                    jnp.where(order_of_lane == 2, pick(k + 2), pick(k + 3)),
                )
                scale, back = choose(0), choose(4)
                scale, back = jnp.concatenate([scale, scale], axis=0), jnp.concatenate([back, back], axis=0)
                new = []
                for u, store in ((0, legendre0), (1, legendre1)):
                    cols = slice(128 * u, 128 * u + 128)
                    last, before = carry[2 * u], carry[2 * u + 1]
                    start = jnp.where(mapsv[16:, cols] + first == l.astype(F32), diagv[:, cols], 0.0)
                    value = (scale * mapsv[:16, cols]) * last + (start - back * before)
                    store[pl.ds(l, 16, stride=NLAT), :] = value
                    new += [value, last]
                carry = tuple(new)
            return carry

        if h == 0:
            carry = (jnp.zeros((16, 128), F32),) * 4
        carry = lax.fori_loop(0, 4 if h == 0 else 2, degrees, carry)

    def finish(v, _):
        rows = pl.ds(pl.multiple_of((4 * (v // GROUPS) + lax.rem(v, GROUPS)) * NLAT, NLAT), NLAT)
        for u, store in ((0, legendre0), (1, legendre1)):
            part = store[rows, :].astype(BF16)
            table[v, :, 128 * u : 128 * u + 128] = part
        return 0

    lax.fori_loop(0, Q * GROUPS, finish, 0)

    for load in loads[5:]:
        load.wait()
    weights = weightv[...].T
    rotated[0] = jnp.where(low, weights, half(weights))
    rotated[1] = jnp.where(low, -half(weights), weights)
    coeffs[...] = jnp.zeros_like(coeffs)
    dcoeffs[...] = jnp.zeros_like(dcoeffs)

    order_of_row = lax.broadcasted_iota(jnp.int32, (256, 128), 0) % 16 // 4
    upper = lax.broadcasted_iota(jnp.int32, (1, 8, 128), 1) < 4
    tile = lambda g: pl.ds(g * 16, 16)

    def analyse(phase, q, into):
        whole(phase, q).wait_recv()

        def one(g, _):
            block = recv[phase, q, :, tile(g), :].reshape(256, 128)
            zero = jnp.zeros_like(block)
            spread = jnp.concatenate([jnp.where(order_of_row == k, block, zero) for k in range(4)], axis=1)
            into[g] = into[g] + jnp.dot(table[GROUPS * q + g], spread, preferred_element_type=F32)
            return 0

        for g in range(GROUPS):
            one(g, 0)
        return 0

    def synthesize(phase, q, scaled):
        def one(g, _):
            out = jnp.dot(table_t[GROUPS * q + g], filtered[g], preferred_element_type=F32)
            parts = [out[:, 128 * k : 128 * k + 128].reshape(N, 2, 8, 128) for k in range(4)]
            first_half = jnp.where(upper, parts[0][:, 0], parts[1][:, 0])
            second_half = jnp.where(upper, parts[2][:, 1], parts[3][:, 1])
            out = jnp.concatenate([first_half, second_half], axis=1)
            if scaled:
                out = out * colwv[q].reshape(N, 16, 128)
            send[phase, q, :, tile(g), :] = out.astype(BF16)
            return 0

        for g in range(GROUPS):
            one(g, 0)
        ship(phase, q)
        return 0

    def turn_table(v, _):
        table_t[v] = table[v].T
        return 0

    def forward_chunk(q, _):
        analyse(0, q, coeffs)

        @pl.when(q == 1)
        def _():
            lax.fori_loop(0, Q * GROUPS, turn_table, 0)

        return 0

    lax.fori_loop(0, Q, forward_chunk, 0)

    def filter_group(g, _):
        for k in range(4):
            cols = slice(128 * k, 128 * k + 128)
            value = coeffs[g, :, cols]
            filtered[g, :, cols] = (rotated[0] * value + rotated[1] * half(value)).astype(BF16)
        return 0

    for g in range(GROUPS):
        filter_group(g, 0)
    lax.fori_loop(0, Q, lambda q, _: synthesize(1, q, False), 0)
    for g in range(GROUPS):
        for k in range(4):
            turned[g, :, 128 * k : 128 * k + 128] = half(coeffs[g, :, 128 * k : 128 * k + 128])

    def gather(phase, q):
        whole(phase, q).wait_recv()
        stage[...] = recv[phase, q].reshape(N * PART, 128).astype(F32)
        for r in range(4):
            turned = stage[pl.ds(r, NLAT, stride=4), :].astype(BF16).T
            tt[0, WIDTH * r : WIDTH * r + WIDTH, :] = turned[:WIDTH]
            tt[1, WIDTH * r : WIDTH * r + WIDTH, :] = turned[WIDTH:]

    def grid_rows(factors):
        return jnp.dot(tt[0], factors[:NLAT, :], preferred_element_type=F32) + jnp.dot(
            tt[1], factors[NLAT:, :], preferred_element_type=F32
        )

    def activation(q, _):
        gather(1, q)
        prev[...] = grid_rows(gtv)

        def strip(i, _):
            here = pl.ds(pl.multiple_of(i * 16, 16), 16)
            there = pl.ds(pl.multiple_of(q * 256 + i * 16, 16), 16)
            pre = prev[here, :]
            cdf = 0.5 + 0.5 * lax.erf(pre * (1.0 / math.sqrt(2.0)))
            density = jnp.exp(-0.5 * pre * pre) * (1.0 / math.sqrt(2.0 * math.pi))
            act_ref[there, :] = (pre * cdf).astype(BF16)
            dprev[there, :] = (cotv[there, :].astype(F32) * (cdf + pre * density)).astype(BF16)
            return 0

        lax.fori_loop(0, 16, strip, 0)
        fourier(2, q, dprev, gtv, False)
        ship(2, q)
        return 0

    lax.fori_loop(0, Q, activation, 0)

    lax.fori_loop(0, Q, lambda q, _: analyse(2, q, dcoeffs), 0)

    places = [(g, slice(None), slice(128 * k, 128 * k + 128)) for g in range(GROUPS) for k in range(4)]
    same = sum(dcoeffs[place] * coeffs[place] for place in places)
    cross = sum(dcoeffs[place] * turned[place] for place in places)
    partial = jnp.where(low, same + half(same), cross - half(cross)).astype(BF16)
    gsend[:ROWS] = partial.reshape(ROWS, 16, 128)
    gsend[ROWS:] = jnp.zeros((N - ROWS, 16, 128), BF16)

    def small_copy(turn, peer):
        return pltpu.make_async_remote_copy(
            src_ref=gout if turn else gsend.at[peer], dst_ref=(gall if turn else grecv).at[me],
            send_sem=send_r.at[turn], recv_sem=recv_r.at[turn],
            device_id=(dp, peer), device_id_type=MESH,
        )

    def small_whole(turn):
        ref = (gall if turn else grecv).at[pl.ds(0, N - 1)]
        return pltpu.make_async_remote_copy(
            src_ref=gsend.at[pl.ds(0, N - 1)], dst_ref=ref, send_sem=send_r.at[turn], recv_sem=recv_r.at[turn],
            device_id=(dp, peers[0]), device_id_type=MESH,
        )

    for peer in peers:
        small_copy(0, peer).start()
    grecv[me] = gsend[me]
    def adjoint_group(g, _):
        for k in range(4):
            cols = slice(128 * k, 128 * k + 128)
            value = dcoeffs[g, :, cols]
            filtered[g, :, cols] = (rotated[0] * value - rotated[1] * half(value)).astype(BF16)
        return 0

    for g in range(GROUPS):
        adjoint_group(g, 0)
    synthesize(3, 0, True)

    synthesize(3, 1, True)
    synthesize(3, 2, True)
    small_whole(0).wait_recv()
    total = (jnp.sum(grecv[...].astype(F32), axis=0) * (1.0 / NLAT)).astype(BF16)
    gout[...] = total
    gall[me] = total
    for peer in peers:
        small_copy(1, peer).start()

    def gradient(q, _):
        gather(3, q)
        gf_ref[quad(q), :] = grid_rows(ftv).astype(BF16)
        return 0

    lax.fori_loop(0, Q, gradient, 0)

    small_whole(1).wait_recv()
    gw_ref[...] = gall[:ROWS].reshape(NLAT, 128).astype(F32).T

    for phase in range(4):
        for q in range(Q):
            whole(phase, q).wait_send()
    for turn in range(2):
        small_whole(turn).wait_send()


def hand_over(act, gf, gw, act_out, gf_out, gw_out, sems):
    moves = ((act, act_out), (gf, gf_out), (gw, gw_out))
    copies = [pltpu.make_async_copy(src, dst, sems.at[i]) for i, (src, dst) in enumerate(moves)]
    for copy in copies:
        copy.start()
    for copy in copies:
        copy.wait()


def shards(fields, filter_weight, cotangent):
    rows, width, nlon = fields.shape
    if (rows, width, nlon) != (ROWS, WIDTH, NLON) or lax.axis_size("spatial") != N:
        raise ValueError("unexpected sizes")
    held = constants()
    names = ("forward", "inverse", "row_weights", "col_weights", "maps", "diag", "coef")
    flat = rows * width
    dma, vmem = pltpu.SemaphoreType.DMA, pltpu.VMEM
    shapes = (
        jax.ShapeDtypeStruct((flat, nlon), BF16),
        jax.ShapeDtypeStruct((flat, nlon), BF16),
        jax.ShapeDtypeStruct((2 * width, NLAT), F32),
    )
    results = pl.pallas_call(
        kernel,
        out_shape=tuple(vmem(shape.shape, shape.dtype) for shape in shapes),
        in_specs=[pl.BlockSpec(memory_space=pl.ANY)] * 10,
        out_specs=(pl.BlockSpec(memory_space=pltpu.VMEM),) * 3,
        scratch_shapes=[
            vmem((flat, nlon), BF16), vmem((flat, nlon), BF16), vmem((2 * width, NLAT), F32),
            vmem((2 * NLAT, nlon), BF16), vmem((2 * NLAT, nlon), BF16), vmem((16, 128), F32),
            vmem((Q, 256, 128), F32), vmem((32, 256), F32), vmem((16, 256), F32), vmem((64, 256), F32),
            vmem((N * PART, 128), F32), vmem((4, Q, N, PART, 128), BF16), vmem((4, Q, N, PART, 128), BF16),
            vmem((16 * NLAT, 128), F32), vmem((16 * NLAT, 128), F32),
            vmem((Q * GROUPS, NLAT, 256), BF16), vmem((Q * GROUPS, 256, NLAT), BF16),
            vmem((GROUPS, NLAT, 512), F32), vmem((GROUPS, NLAT, 512), F32), vmem((GROUPS, NLAT, 512), F32), vmem((GROUPS, NLAT, 512), BF16),
            vmem((2, NLAT, 128), F32), vmem((256, nlon), F32),
            vmem((2, 256, NLAT), BF16), vmem((flat, nlon), BF16),
            vmem((N, 16, 128), BF16), vmem((N, 16, 128), BF16), vmem((16, 128), BF16), vmem((N, 16, 128), BF16),
            dma((12,)), dma((4, Q)), dma((4, Q)), dma((2,)), dma((2,)),
        ],
        compiler_params=pltpu.CompilerParams(
            collective_id=0, has_side_effects=True, vmem_limit_bytes=56 << 20
        ),
    )(
        fields.reshape(flat, nlon), cotangent.reshape(flat, nlon), filter_weight.reshape(2 * width, NLAT),
        *(jnp.asarray(held[name]) for name in names),
    )
    activated, grad_fields, grad_weight = pl.pallas_call(
        hand_over,
        out_shape=shapes,
        in_specs=[pl.BlockSpec(memory_space=pltpu.VMEM)] * 3,
        out_specs=(pl.BlockSpec(memory_space=pl.ANY),) * 3,
        scratch_shapes=[dma((3,))],
    )(*(pltpu.with_memory_space_constraint(result, pltpu.VMEM) for result in results))
    return (
        activated.reshape(rows, width, nlon), grad_fields.reshape(rows, width, nlon),
        grad_weight.reshape(2, width, NLAT),
    )


def solution(mesh):
    in_specs = (P("spatial", "dp", None), P(None, "dp", None), P("spatial", "dp", None))
    out_specs = (P("spatial", "dp", None), P("spatial", "dp", None), P(None, "dp", None))
    return jax.shard_map(shards, mesh=mesh, in_specs=in_specs, out_specs=out_specs, check_vma=False)
```
